128 devices in a mesh: leaf: 16 (over y, z), front: 8 (over x, core).
Axes of the slice: x: 4, y: 4, z: 4, core: 2. Of those that a mesh axis runs over, the one named last changes fastest.
Arguments:
- sub_rhs: float32 [393216, 128], P(('leaf', 'front')), may hold values from -6 to 6
- sub_dinv: float32 [3072, 128, 128], P(('leaf', 'front')), as said below
- sub_off: float32 [2944, 2, 128, 128], P(('leaf', 'front')), may hold values from -0.25 to 0.25
- sub_pattern: int32 [2944, 2], P(('leaf', 'front')), may hold values from 0 to 22, as said below
- sub_update: float32 [32768, 3072], P(('leaf', 'front')), may hold values from -0.0546875 to 0.0546875
- sub_map: int32 [128, 2], replicated, may hold values from 0 to 31, as said below
- front_rhs: float32 [63488, 128], P(('leaf', 'front')), may hold values from -6 to 6
- piv_inverse: float32 [63488, 2048], P(('leaf', 'front')), as said below
- upd_factor: float32 [61440, 2048], P(('leaf', 'front')), may hold values from -0.0625 to 0.0625
- front_map: int32 [30, 16], replicated, may hold values from 0 to 31, as said below
Outputs:
- sub_solution: float32 [393216, 128], P(('leaf', 'front'))
- front_solution: float32 [63488, 128], P(('leaf', 'front'))
The draws below stay inside these ranges and needn't reach their ends.
Inputs may be any that keep to these rules, and one draw needn't show every extreme that they name: `sub_pattern`: in entry row i - 1 of a subtree (its block row i) the first index is i - 1 and every index is below i. `sub_map`: each row names 2 different blocks of a level-1 front. `front_map`: rows are ordered by level, then by front; each row names 16 different parent blocks, and the last two rows (children of the root) name only the 16 pivot blocks. `sub_dinv`: each inverse diagonal block is full. `piv_inverse`: each front's inverse pivot block is lower triangular with a unit diagonal.
All inputs are finite; a program needn't handle non-finite values.
Results may differ from the reference program's by a relative error of at most 0.0001.
Values sent between devices are 32-bit elements; how exact they have to be, the bound alone decides.
A program may use at most 128 MiB of HBM per device.

```python
import math
import jax
import jax.numpy as jnp
from jax import lax

B = 128
NRHS = 128
P_SIZE = 2048
U = 2048
SB = 24
USB = 2
K = 2
LEVELS = 5
PB = 16
UB = 16
PROWS = 496
UROWS = 480
MAPROWS = 30
N_LEAF = 16
N_FRONT = 8


def draw_sub_dinv(key, part):
    shape = (N_LEAF * N_FRONT * SB, B, B)
    noise_values = jax.random.normal(key, shape, jnp.float32)
    return jnp.eye(B, dtype=jnp.float32)[None, :, :] + 0.35 * noise_values / math.sqrt(B)


def draw_piv_inverse(key, part):
    total = N_LEAF * N_FRONT * PROWS
    row_ids = jnp.arange(total)
    device_ids = row_ids // PROWS
    local_row = row_ids % PROWS
    leaf_ids = device_ids // N_FRONT
    front_ids = device_ids % N_FRONT
    node_row = jnp.zeros((total,), jnp.int32)
    offset = 0
    for level in range(1, LEVELS + 1):
        group_span = 2 ** (level - 1)
        piv_rows = P_SIZE // (N_FRONT * group_span)
        inside = (local_row >= offset) & (local_row < offset + piv_rows)
        my_rank = leaf_ids % group_span * N_FRONT + front_ids
        node_row = jnp.where(inside, my_rank * piv_rows + local_row - offset, node_row)
        offset += piv_rows
    column_ids = jnp.arange(P_SIZE)
    noise_values = jax.random.normal(key, (total, P_SIZE), jnp.float32)
    noise_values = noise_values / math.sqrt(P_SIZE)
    lower = column_ids[None, :] < node_row[:, None]
    diagonal = (column_ids[None, :] == node_row[:, None]).astype(jnp.float32)
    return jnp.where(lower, noise_values, 0.0) + diagonal


def draw_sub_pattern(key, part):
    total = N_LEAF * N_FRONT * (SB - 1)
    block_row = jnp.arange(total) % (SB - 1) + 1
    others = jax.random.randint(key, (total, K - 1), 0, block_row[:, None])
    return jnp.concatenate([(block_row - 1)[:, None], others], axis=1).astype(jnp.int32)


def distinct_blocks(key, count_rows, limit_rows):
    scores = jax.random.randint(key, (count_rows, PB + UB), 0, 2 ** 20)
    positions = jnp.arange(PB + UB)
    scores = scores * (PB + UB) + positions[None, :]
    scores = jnp.where((positions[None, :] >= PB) & limit_rows[:, None], scores + 2 ** 30, scores)
    ordering = jnp.argsort(scores, axis=1, stable=True)
    return ordering.astype(jnp.int32)


def draw_sub_map(key, part):
    count_rows = N_LEAF * N_FRONT
    ordering = distinct_blocks(jax.random.fold_in(key, 11), count_rows, jnp.zeros((count_rows,), bool))
    return ordering[:, :USB]


def draw_front_map(key, part):
    count_rows = MAPROWS
    limit_rows = jnp.arange(count_rows) >= count_rows - 2
    ordering = distinct_blocks(jax.random.fold_in(key, 23), count_rows, limit_rows)
    return ordering[:, :UB]


def levels(stream_key, extent, cuts, smallest, top_value):
    def one(axis_at, shards_of):
        draws = jax.random.uniform(jax.random.fold_in(jax.random.fold_in(stream_key, 6), axis_at), (shards_of,), jnp.float32, smallest / len(cuts), top_value / len(cuts))
        return jnp.repeat(jnp.exp(draws), extent[axis_at] // shards_of).reshape((-1,) + (1,) * (len(extent) - axis_at - 1))

    loudness = one(*cuts[0])
    for cut in cuts[1:]:
        loudness = loudness * one(*cut)
    return loudness


def gaussian(stream_key, dims, width, most, pieces=(), kind=jnp.bfloat16):
    values = jax.random.normal(stream_key, dims, jnp.float32) * width
    if len(pieces) > 0:
        values = levels(stream_key, dims, pieces, -0.22, 0.18) * values
    return jnp.clip(values, min=-most, max=most).astype(kind)


def setup_inputs(seed: int = 0) -> dict:
    key_of = jax.random.split(jax.random.key(seed), 11)
    sub_rhs = gaussian(key_of[0], (N_LEAF * N_FRONT * SB * B, NRHS), 1.0, 6.0, ((0, 128),), jnp.float32)
    sub_dinv = draw_sub_dinv(jax.random.fold_in(key_of[10], 71), 0)
    sub_off = gaussian(key_of[2], (N_LEAF * N_FRONT * (SB - 1), K, B, B), (2 * K * B) ** -0.5, 0.25, ((0, 128),), jnp.float32)
    sub_pattern = draw_sub_pattern(jax.random.fold_in(key_of[10], 71), 0)
    sub_update = gaussian(key_of[4], (N_LEAF * N_FRONT * USB * B, SB * B), (4 * SB * B) ** -0.5, 0.0546875, ((0, 128),), jnp.float32)
    sub_map = draw_sub_map(jax.random.fold_in(key_of[10], 71), 0)
    front_rhs = gaussian(key_of[6], (N_LEAF * N_FRONT * PROWS, NRHS), 1.0, 6.0, ((0, 128),), jnp.float32)
    piv_inverse = draw_piv_inverse(jax.random.fold_in(key_of[10], 71), 0)
    upd_factor = gaussian(key_of[8], (N_LEAF * N_FRONT * UROWS, P_SIZE), (4 * P_SIZE) ** -0.5, 0.0625, ((0, 128),), jnp.float32)
    front_map = draw_front_map(jax.random.fold_in(key_of[10], 71), 0)
    return {"sub_rhs": sub_rhs, "sub_dinv": sub_dinv, "sub_off": sub_off, "sub_pattern": sub_pattern, "sub_update": sub_update, "sub_map": sub_map, "front_rhs": front_rhs, "piv_inverse": piv_inverse, "upd_factor": upd_factor, "front_map": front_map}


def solve_subtree(operands):
    right_side, diag_inverse, off_blocks, pattern, update_rows = operands
    highest = lax.Precision.HIGHEST
    blocks = right_side.reshape(SB, B, NRHS)
    solved = jnp.zeros((SB, B, NRHS), jnp.float32)
    solved = solved.at[0].set(jnp.dot(diag_inverse[0], blocks[0], precision=highest, preferred_element_type=jnp.float32))

    def advance(block_id, solved):
        remain = blocks[block_id]
        for which in range(K):
            remain = remain - jnp.dot(off_blocks[block_id - 1, which], solved[pattern[block_id - 1, which]], precision=highest, preferred_element_type=jnp.float32)
        return solved.at[block_id].set(jnp.dot(diag_inverse[block_id], remain, precision=highest, preferred_element_type=jnp.float32))

    solved = lax.fori_loop(1, SB, advance, solved)
    flat_rows = solved.reshape(SB * B, NRHS)
    return flat_rows, -jnp.dot(update_rows, flat_rows, precision=highest, preferred_element_type=jnp.float32)


def take_level(array, offset, count, num_nodes, group_span):
    piece = array[:, :, offset:offset + count]
    return piece.reshape(num_nodes, group_span * N_FRONT * count, array.shape[3])


def reference(sub_rhs, sub_dinv, sub_off, sub_pattern, sub_update, sub_map, front_rhs, piv_inverse, upd_factor, front_map):
    highest = lax.Precision.HIGHEST
    devices_all = N_LEAF * N_FRONT
    sub_y, sub_w = lax.map(solve_subtree, (sub_rhs.reshape(devices_all, SB * B, NRHS), sub_dinv.reshape(devices_all, SB, B, B), sub_off.reshape(devices_all, SB - 1, K, B, B), sub_pattern.reshape(devices_all, SB - 1, K), sub_update.reshape(devices_all, USB * B, SB * B)))
    child_blocks = sub_w.reshape(N_LEAF, N_FRONT * USB, B, NRHS)
    child_maps = sub_map.reshape(N_LEAF, N_FRONT * USB)
    onehot = (child_maps[:, :, None] == jnp.arange(PB + UB)[None, None, :]).astype(jnp.float32)
    contrib = jnp.einsum('ncb,ncrs->nbrs', onehot, child_blocks, precision=highest).reshape(N_LEAF, (PB + UB) * B, NRHS)
    rhs_view = front_rhs.reshape(N_LEAF, N_FRONT, PROWS, NRHS)
    piv_view = piv_inverse.reshape(N_LEAF, N_FRONT, PROWS, P_SIZE)
    upd_view = upd_factor.reshape(N_LEAF, N_FRONT, UROWS, P_SIZE)
    results = []
    piv_offset = 0
    upd_offset = 0
    map_offset = 0
    for level in range(1, LEVELS + 1):
        group_span = 2 ** (level - 1)
        num_nodes = N_LEAF // group_span
        piv_rows = P_SIZE // (N_FRONT * group_span)
        pivot_side = take_level(rhs_view, piv_offset, piv_rows, num_nodes, group_span) + contrib[:, :P_SIZE]
        update_side = contrib[:, P_SIZE:]
        inverse_rows = take_level(piv_view, piv_offset, piv_rows, num_nodes, group_span)
        solution = jnp.einsum('nij,njs->nis', inverse_rows, pivot_side, precision=highest)
        results.append(solution.reshape(N_LEAF, N_FRONT, piv_rows, NRHS))
        if level < LEVELS:
            upd_rows = U // (N_FRONT * group_span)
            factor_rows = take_level(upd_view, upd_offset, upd_rows, num_nodes, group_span)
            update = update_side - jnp.einsum('nij,njs->nis', factor_rows, solution, precision=highest)
            parent_blocks = PB + UB if level + 1 < LEVELS else PB
            level_maps = front_map[map_offset:map_offset + num_nodes]
            onehot = (level_maps[:, :, None] == jnp.arange(parent_blocks)[None, None, :]).astype(jnp.float32)
            placed = jnp.einsum('ncb,ncrs->nbrs', onehot, update.reshape(num_nodes, UB, B, NRHS), precision=highest)
            contrib = placed.reshape(num_nodes // 2, 2, parent_blocks * B, NRHS).sum(axis=1)
            upd_offset += upd_rows
            map_offset += num_nodes
        piv_offset += piv_rows
    front_solution = jnp.concatenate(results, axis=2).reshape(N_LEAF * N_FRONT * PROWS, NRHS)
    return sub_y.reshape(N_LEAF * N_FRONT * SB * B, NRHS), front_solution
```

```python
import jax
import jax.numpy as jnp
from jax import lax
from jax.experimental import pallas as pl
from jax.experimental.pallas import tpu as pltpu
from jax.sharding import PartitionSpec as P

B = 128
N = 128
SB = 24
K = 2
ROWS = 2048
PB = 16
LEVELS = 5
PROWS = 496
UROWS = 480
MAPROWS = 30
YS = (1, 1, 1, 2, 4)
ZS = (1, 2, 4, 4, 4)
HELD = (256, 128, 64, 32, 16)
MAP_AT = (0, 16, 24, 28)
ENTRY_AT = (None, 0, 18, 35, 52, 69)
ORDER = ("xzy", "yzx")
DIM_AT = {"x": 0, "z": 3, "y": 6}
COPIES = 19
F32 = jnp.float32
BF16 = jnp.bfloat16


def split(value):
    high = value.astype(BF16)
    return high, (value - high.astype(F32)).astype(BF16)


def side(value):
    return jnp.concatenate(split(value), axis=1)


def stack(value):
    return jnp.concatenate(split(value), axis=0)


def dot(left, right):
    return jnp.dot(left, right, preferred_element_type=F32)


def fold(product):
    half = product.shape[0] // 2
    return product[:half, :N] + (product[:half, N:] + product[half:, :N])


class Gather:
    def __init__(self, buf, send, recv, level, at):
        self.buf, self.send, self.recv, self.at = buf, send, recv, at
        self.size = {"x": 4, "z": ZS[level - 1], "y": YS[level - 1]}
        self.own = {
            d: 0 if self.size[d] == 1 else at[d] % self.size[d] for d in "yzx"
        }

    def dims(self, core):
        return [d for d in ORDER[core] if self.size[d] > 1]

    def view(self, full, own, core):
        index = [slice(None) if d in full else own[d] for d in "yzx"]
        return self.buf.at[index[0], index[1], index[2], core]

    def offsets(self, dim):
        return (2, 1, 3) if self.size[dim] == 4 else (1,)

    def moved(self, dim, offset):
        here = self.at[dim]
        if self.size[dim] == 4:
            return (here + offset) % 4
        return here + 1 - 2 * (here % 2)

    def copy(self, view, which, **changes):
        place = {**self.at, **changes}
        return pltpu.make_async_remote_copy(
            src_ref=view,
            dst_ref=view,
            send_sem=self.send.at[which],
            recv_sem=self.recv.at[which],
            device_id=(place["y"] * 4 + place["z"], place["x"] * 2 + place["core"]),
            device_id_type=pl.DeviceIdType.MESH,
        )

    def outgoing(self, phase, core):
        dims = self.dims(core)
        dim = dims[phase]
        view = self.view(dims[:phase], self.own, core)
        return [
            self.copy(view, DIM_AT[dim] + offset - 1, core=core, **{dim: self.moved(dim, offset)})
            for offset in self.offsets(dim)
        ]

    def incoming(self, phase, core):
        dims = self.dims(core)
        dim = dims[phase]
        found = []
        for offset in self.offsets(dim):
            origin = self.moved(dim, 4 - offset) % self.size[dim]
            view = self.view(dims[:phase], {**self.own, dim: origin}, core)
            found.append((view, DIM_AT[dim] + offset - 1))
        return found

    def shared(self, core):
        views = [self.view((), self.own, core)]
        for phase in range(len(self.dims(core))):
            views += [view for view, _ in self.incoming(phase, core)]
        return views

    def crossing(self, core, to, first=0, many=COPIES):
        views = list(enumerate(self.shared(core)))[first : first + many]
        return [self.copy(view, 9 + which, core=to) for which, view in views]

    def start(self, core):
        for copy in self.outgoing(0, core):
            copy.start()
        for copy in self.crossing(core, 1 - core, 0, 1):
            copy.start()

    def phases(self, core):
        return len(self.dims(core))

    def advance(self, phase, core):
        if phase >= self.phases(core):
            return
        first = 1 + sum(len(self.incoming(p, core)) for p in range(phase))
        arrivals = self.incoming(phase, core)
        for view, which in arrivals:
            self.copy(view, which, core=1 - core).wait_recv()
        if phase + 1 < self.phases(core):
            for copy in self.outgoing(phase + 1, core):
                copy.start()
        for copy in self.crossing(core, 1 - core, first, len(arrivals)):
            copy.start()

    def finish(self, core):
        for copy in self.crossing(1 - core, 1 - core):
            copy.wait_recv()

    def drain(self, core):
        for phase in range(self.phases(core)):
            for copy in self.outgoing(phase, core):
                copy.wait_send()
        for copy in self.crossing(core, 1 - core):
            copy.wait_send()


def kernel(
    pattern, spots, hits,
    rhs, dinv, off, update, front_rhs, piv, factor,
    solved_out, front_out,
    b_v, d_v, l_v, u_v, m_v, e_v, y_v, yhl_v, g_v, c_v, acc_v, p_v, last_v,
    h1, h2, h3, h4, h5, w0, w1, w2, w3, w4, z1, z2, z3, z4,
    load_sem, store_sem, send, recv,
):
    leaf = lax.axis_index("leaf")
    front = lax.axis_index("front")
    core = front % 2
    at = {"y": leaf // 4, "z": leaf % 4, "x": front // 2, "core": core}

    def both(step):
        for which in (0, 1):
            @pl.when(core == which)
            def _():
                step(which)

    bufs = (h1, h2, h3, h4, h5, w0, w1, w2, w3, w4, z1, z2, z3, z4)
    groups = (1, 2, 3, 4, 5, 1, 2, 3, 4, 5, 1, 2, 3, 4)
    gathers = [
        Gather(buf, send.at[g], recv.at[g], level, at)
        for g, (buf, level) in enumerate(zip(bufs, groups))
    ]
    hs, ws, zs = gathers[:5], gathers[5:10], gathers[10:]

    def mine(gather):
        own = gather.own
        return (own["y"], own["z"], own["x"], core)

    loads = []

    def load(source, target):
        copy = pltpu.make_async_copy(source, target, load_sem.at[len(loads)])
        copy.start()
        loads.append(copy)

    load(dinv, d_v)
    load(off, l_v)
    load(rhs, b_v)
    row = 0
    for gather, held in zip(hs, HELD):
        load(front_rhs.at[pl.ds(row, held)], gather.buf.at[mine(gather)])
        row += held
    load(update, u_v)
    load(piv, m_v)
    load(factor, e_v)

    barrier = pltpu.get_barrier_semaphore()
    for dim in "xzy":
        for offset in (1, 2, 3):
            place = {**at, dim: (at[dim] + offset) % 4}
            pl.semaphore_signal(
                barrier,
                inc=1,
                device_id=(place["y"] * 4 + place["z"], place["x"] * 2 + core),
                device_id_type=pl.DeviceIdType.MESH,
            )
    pl.semaphore_signal(
        barrier, inc=1, device_id=(leaf, at["x"] * 2 + 1 - core), device_id_type=pl.DeviceIdType.MESH
    )
    pl.semaphore_wait(barrier, 10)

    for copy in loads[3:8]:
        copy.wait()
    both(lambda c: [gather.start(c) for gather in hs])
    for copy in loads[:3]:
        copy.wait()
    loads[8].wait()

    def prepare(block, slot):
        high, low = split(d_v[block])
        wide = jnp.concatenate([l_v[block - 1, 0], l_v[block - 1, 1], b_v[block]], axis=1)
        wide_high, wide_low = split(wide)
        first = dot(jnp.concatenate([high, low], axis=0), wide_high)
        product = first[:B] + (first[B:] + dot(high, wide_low))
        g_v[slot] = stack(product[:, : 2 * B])
        c_v[slot] = product[:, 2 * B :]

    def keep(block, value):
        y_v[block] = value
        yhl_v[block] = side(value)

    def couple(block):
        columns = pl.ds(pl.multiple_of(block * B, B), B)
        acc_v[...] += fold(dot(stack(u_v[:, columns]), yhl_v[block]))

    keep(0, fold(dot(stack(d_v[0]), side(b_v[0]))))
    prepare(1, 1)
    acc_v[...] = jnp.zeros_like(acc_v)

    def advance(block, carry):
        slot = lax.rem(block, 2)
        known = jnp.concatenate([yhl_v[block - 1], yhl_v[pattern[block - 1, 1]]], axis=0)
        value = c_v[slot] - fold(dot(g_v[slot], known))
        couple(block - 1)
        prepare(jnp.minimum(block + 1, SB - 1), 1 - slot)
        keep(block, value)
        return carry

    bounds = (1, 7, 13, 19, SB)
    for phase in range(4):
        lax.fori_loop(bounds[phase], bounds[phase + 1], advance, 0)
        if phase < 3:
            both(lambda c: [gather.advance(phase, c) for gather in hs])
    couple(SB - 1)

    stores = []

    def store(source, target):
        copy = pltpu.make_async_copy(source, target, store_sem.at[len(stores)])
        copy.start()
        stores.append(copy)

    def run(gather, before):
        both(gather.start)
        before()
        for phase in range(3):
            both(lambda c: gather.advance(phase, c))
        both(gather.finish)

    def fill(level):
        gather = hs[level - 1]
        both(gather.finish)
        held = HELD[level - 1]
        many = 8 * held
        for y in range(YS[level - 1]):
            for z in range(ZS[level - 1]):
                first = (y * ZS[level - 1] + z) * many
                p_v[first : first + many, :] = gather.buf[y, z].reshape(many, N)

    w0_at = mine(ws[0])
    w0[w0_at] = -acc_v[...]

    def before_first():
        store(y_v, solved_out)
        fill(1)
        loads[9].wait()
        loads[10].wait()

    run(ws[0], before_first)

    w0_blocks = w0.reshape(PB, B, N)

    def landed(entry):
        total = hits[entry, 0] * w0_blocks[spots[entry, 0]]
        for s in range(1, 8):
            total = total + hits[entry, s] * w0_blocks[spots[entry, s]]
        return total

    def place_first(block, carry):
        rows = pl.ds(pl.multiple_of(block * B, B), B)
        p_v[rows, :] = p_v[rows, :] + landed(block)
        return carry

    lax.fori_loop(0, PB, place_first, 0)

    def place(level):
        blocks = ws[level - 1].buf.reshape(2 * PB, B, N)

        def body(block, carry):
            rows = pl.ds(pl.multiple_of(block * B, B), B)
            entry = ENTRY_AT[level] + block
            total = p_v[rows, :]
            for child in (0, 1):
                total = total + hits[entry, child] * blocks[spots[entry, child]]
            p_v[rows, :] = total
            return carry

        lax.fori_loop(0, PB, body, 0)

    def update_rows(level):
        if level == 1:
            return jnp.concatenate([landed(PB), landed(PB + 1)], axis=0)
        held = HELD[level - 1]
        pieces = ws[level - 1].buf.reshape(2 * ROWS // held, held, N)
        entry = ENTRY_AT[level] + PB
        return (
            hits[entry, 0] * pieces[spots[entry, 0]] + hits[entry, 1] * pieces[spots[entry, 1]]
        )

    def multiply(matrix, row, held, chunks):
        tall = min(held, B)
        totals = []
        for first in range(0, held, tall):
            total = None
            column = 0
            for right in chunks:
                depth = right.shape[0]
                left = stack(matrix[row + first : row + first + tall, column : column + depth])
                part = dot(left, right)
                total = part if total is None else total + part
                column += depth
            totals.append(fold(total))
        return totals[0] if len(totals) == 1 else jnp.concatenate(totals, axis=0)

    piv_row = 0
    upd_row = 0
    for level in range(1, LEVELS + 1):
        held = HELD[level - 1]
        value = multiply(m_v, piv_row, held, [side(p_v[...])])
        if level == LEVELS:
            last_v[...] = value
            store(last_v, front_out.at[pl.ds(piv_row, held)])
            break
        gather = zs[level - 1]
        at_own = mine(gather)
        gather.buf[at_own] = value

        def before_solution(level=level, gather=gather, row=piv_row, held=held):
            store(gather.buf.at[mine(gather)], front_out.at[pl.ds(row, held)])
            fill(level + 1)

        run(gather, before_solution)
        chunks = [
            side(gather.buf[y, z].reshape(8 * held, N))
            for y in range(YS[level - 1])
            for z in range(ZS[level - 1])
        ]
        below = update_rows(level) - multiply(e_v, upd_row, held, chunks)
        wide = ws[level]
        wide_at = mine(wide)
        wide.buf[wide_at] = below
        run(wide, lambda: None)
        place(level + 1)
        piv_row += held
        upd_row += held

    both(lambda c: [gather.drain(c) for gather in gathers])
    for copy in stores:
        copy.wait()


def tables(sub_map, front_map):
    leaf = lax.axis_index("leaf")
    front = lax.axis_index("front")
    pivots = jnp.arange(PB, dtype=jnp.int32)
    places, flags = [], []
    maps = lax.dynamic_slice_in_dim(sub_map, leaf * 8, 8)
    wanted = jnp.concatenate([pivots, PB + 2 * front + jnp.arange(2, dtype=jnp.int32)])
    match = maps[None] == wanted[:, None, None]
    places.append(2 * jnp.arange(8, dtype=jnp.int32) + match[:, :, 1].astype(jnp.int32))
    flags.append(match.any(axis=2))
    for level in range(2, LEVELS + 1):
        held = HELD[level - 1]
        maps = lax.dynamic_slice_in_dim(
            front_map, MAP_AT[level - 2] + 2 * (leaf // 2 ** (level - 1)), 2
        )
        row = ((leaf % 2 ** (level - 1)) * 8 + front) * held
        wanted = jnp.concatenate([pivots, (PB + row // B)[None]])
        match = maps[None] == wanted[:, None, None]
        place = jnp.sum(match * jnp.arange(PB, dtype=jnp.int32), axis=2, dtype=jnp.int32)
        place = place + jnp.array([0, PB], jnp.int32)
        last = jnp.arange(PB + 1)[:, None] == PB
        place = jnp.where(last, place * (B // held) + row % B // held, place)
        places.append(jnp.pad(place, ((0, 0), (0, 6))))
        flags.append(jnp.pad(match.any(axis=2), ((0, 0), (0, 6))))
    return jnp.concatenate(places), jnp.concatenate(flags).astype(F32)


def per_device(
    sub_rhs, sub_dinv, sub_off, sub_pattern, sub_update, sub_map,
    front_rhs, piv_inverse, upd_factor, front_map,
):
    def wide(level, held):
        return pltpu.VMEM((YS[level - 1], ZS[level - 1], 4, 2, held, N), F32)

    scratch = [
        pltpu.VMEM((SB, B, N), F32),
        pltpu.VMEM((SB, B, B), F32),
        pltpu.VMEM((SB - 1, K, B, B), F32),
        pltpu.VMEM((2 * B, SB * B), F32),
        pltpu.VMEM((PROWS, ROWS), F32),
        pltpu.VMEM((UROWS, ROWS), F32),
        pltpu.VMEM((SB, B, N), F32),
        pltpu.VMEM((SB, B, 2 * N), BF16),
        pltpu.VMEM((2, 2 * B, 2 * B), BF16),
        pltpu.VMEM((2, B, N), F32),
        pltpu.VMEM((2 * B, N), F32),
        pltpu.VMEM((ROWS, N), F32),
        pltpu.VMEM((HELD[-1], N), F32),
    ]
    scratch += [wide(level, HELD[level - 1]) for level in range(1, 6)]
    scratch += [wide(1, 256)]
    scratch += [wide(level + 1, HELD[level - 1]) for level in range(1, 5)]
    scratch += [wide(level, HELD[level - 1]) for level in range(1, 5)]
    scratch += [
        pltpu.SemaphoreType.DMA((11,)),
        pltpu.SemaphoreType.DMA((6,)),
        pltpu.SemaphoreType.DMA((14, COPIES)),
        pltpu.SemaphoreType.DMA((14, COPIES)),
    ]
    smem = pl.BlockSpec(memory_space=pltpu.SMEM)
    hbm = pl.BlockSpec(memory_space=pl.ANY)
    solved, fronts = pl.pallas_call(
        kernel,
        out_shape=(
            jax.ShapeDtypeStruct((SB, B, N), F32),
            jax.ShapeDtypeStruct((PROWS, N), F32),
        ),
        in_specs=[smem] * 3 + [hbm] * 7,
        out_specs=(hbm, hbm),
        scratch_shapes=scratch,
        compiler_params=pltpu.CompilerParams(
            collective_id=0, has_side_effects=True, vmem_limit_bytes=62 * 2**20
        ),
    )(
        sub_pattern, *tables(sub_map, front_map),
        sub_rhs.reshape(SB, B, N), sub_dinv, sub_off, sub_update, front_rhs, piv_inverse, upd_factor,
    )
    return solved.reshape(SB * B, N), fronts


def solution(mesh):
    rows = P(("leaf", "front"), None)
    return jax.shard_map(
        per_device,
        mesh=mesh,
        in_specs=(
            rows,
            P(("leaf", "front"), None, None),
            P(("leaf", "front"), None, None, None),
            rows,
            rows,
            P(),
            rows,
            rows,
            rows,
            P(),
        ),
        out_specs=(rows, rows),
        check_vma=False,
    )
```

```python
import itertools

import jax
import jax.numpy as jnp
from jax import lax
from jax.experimental import pallas as pl
from jax.experimental.pallas import tpu as pltpu
from jax.sharding import PartitionSpec as P

B = 128
N = 128
SB = 24
K = 2
ROWS = 2048
PB = 16
LEVELS = 5
PROWS = 496
UROWS = 480
MAPROWS = 30
YS = (1, 1, 1, 2, 4)
ZS = (1, 2, 4, 4, 4)
HELD = (256, 128, 64, 32, 16)
MAP_AT = (0, 16, 24, 28)
ENTRY_AT = (None, 0, 18, 35, 52, 69)
MIXED = (("x", "zy"), ("zy", "x"))
SAME = (("x", "zy"), ("x", "zy"))
CROSS = 18
COPIES = CROSS + 19
COLUMNS_AT = 86
F32 = jnp.float32
BF16 = jnp.bfloat16


def split(value):
    high = value.astype(BF16)
    return high, (value - high.astype(F32)).astype(BF16)


def side(value):
    return jnp.concatenate(split(value), axis=1)


def stack(value):
    return jnp.concatenate(split(value), axis=0)


def dot(left, right):
    return jnp.dot(left, right, preferred_element_type=F32)


def fold(product):
    half = product.shape[0] // 2
    return product[:half, :N] + (product[:half, N:] + product[half:, :N])


class Gather:
    def __init__(self, buf, send, recv, level, at, order, eager):
        self.buf, self.send, self.recv, self.at = buf, send, recv, at
        self.size = {"x": 4, "z": ZS[level - 1], "y": YS[level - 1]}
        self.order, self.eager = order, eager
        self.own = {d: 0 if self.size[d] == 1 else at[d] % self.size[d] for d in "yzx"}

    def sets(self, core):
        found = ["".join(d for d in dims if self.size[d] > 1) for dims in self.order[core]]
        return found[0] or found[1], found[1] if found[0] else ""

    def hops(self, dims):
        steps = [
            dict(zip(dims, offsets))
            for offsets in itertools.product(*(range(self.size[d]) for d in dims))
            if any(offsets)
        ]
        return sorted(steps, key=lambda step: sum(min(o, self.size[d] - o) for d, o in step.items()))

    def moved(self, dim, offset):
        here = self.at[dim]
        if offset == 0:
            return here
        if self.size[dim] == 4:
            return (here + offset) % 4
        return here + 1 - 2 * (here % 2)

    def origin(self, step):
        return {
            d: self.moved(d, -o % self.size[d]) % self.size[d] for d, o in step.items()
        }

    def view(self, core, full="", **places):
        place = {**self.own, **places}
        index = [slice(None) if d in full else place[d] for d in "yzx"]
        return self.buf.at[index[0], index[1], index[2], core]

    def copy(self, view, which, **changes):
        place = {**self.at, **changes}
        return pltpu.make_async_remote_copy(
            src_ref=view,
            dst_ref=view,
            send_sem=self.send.at[which],
            recv_sem=self.recv.at[which],
            device_id=(place["y"] * 4 + place["z"], place["x"] * 2 + place["core"]),
            device_id_type=pl.DeviceIdType.MESH,
        )

    def to(self, step):
        return {d: self.moved(d, o) for d, o in step.items()}

    def out(self, view, which, core, step):
        return lambda: self.copy(view, which, core=core, **self.to(step))

    def across(self, view, which, core):
        return lambda: self.copy(view, which, core=1 - core)

    def plan(self, core):
        first, second = self.sets(core)
        near, far = self.hops(first), self.hops(second) if second else []
        cross = CROSS
        begin = [self.out(self.view(core), i, core, step) for i, step in enumerate(near)]
        used = len(near)
        mine = [(self.view(core), cross)]
        middle, close = [], []
        held = [{}] + [self.origin(step) for step in near]
        sets = [held[i : i + 1] for i in range(len(held))] if self.eager else [held]
        sends = []
        for group in sets:
            view = self.view(core, **group[0]) if self.eager else self.view(core, first)
            sends.append([self.out(view, used + j, core, step) for j, step in enumerate(far)])
            used += len(far)
        if self.eager:
            begin += sends[0]
        for i, step in enumerate(near):
            view = self.view(core, **held[i + 1])
            mine.append((view, cross + 1 + i))
            after = sends[i + 1] if self.eager else sends[0] if i == len(near) - 1 else []
            middle.append(([(view, i)], after + [self.across(view, cross + 1 + i, core)]))
        if not second:
            middle = [(wait, [start[-1]]) for wait, start in middle]
        for j, step in enumerate(far):
            origin = self.origin(step)
            waits = []
            for g, group in enumerate(sets):
                if self.eager:
                    view = self.view(core, **{**group[0], **origin})
                else:
                    view = self.view(core, first, **origin)
                waits.append((view, len(near) + g * len(far) + j))
            view, which = self.view(core, first, **origin), cross + 1 + len(near) + j
            mine.append((view, which))
            close.append((waits, [self.across(view, which, core)]))
        begin.append(self.across(self.view(core), cross, core))
        return begin, middle, close, mine

    def begin(self, core):
        for make in self.plan(core)[0]:
            make().start()

    def follow(self, steps, core):
        for waits, starts in steps:
            for view, which in waits:
                self.copy(view, which, core=1 - core).wait_recv()
            for make in starts:
                make().start()

    def middle(self, core):
        self.follow(self.plan(core)[1], core)

    def close(self, core):
        self.follow(self.plan(core)[2], core)

    def finish(self, core):
        for view, which in self.plan(1 - core)[3]:
            self.copy(view, which, core=1 - core).wait_recv()

    def drain(self, core):
        begin, middle, close, _ = self.plan(core)
        for make in begin + [make for _, starts in middle + close for make in starts]:
            make().wait_send()


def kernel(
    table,
    rhs, dinv, off, update, front_rhs, piv, factor,
    solved_out, front_out,
    b_v, d_v, l_v, u_v, m_v, e_v, y_v, yhl_v, g_v, c_v, acc_v, p_v, last_v,
    h1, h2, h3, h4, h5, w0, w1, w2, w3, w4, z1, z2, z3, z4,
    load_sem, store_sem, send, recv,
):
    leaf = lax.axis_index("leaf")
    front = lax.axis_index("front")
    core = front % 2
    at = {"y": leaf // 4, "z": leaf % 4, "x": front // 2, "core": core}

    def both(step):
        for which in (0, 1):
            @pl.when(core == which)
            def _():
                step(which)

    bufs = (h1, h2, h3, h4, h5, w0, w1, w2, w3, w4, z1, z2, z3, z4)
    groups = (1, 2, 3, 4, 5, 1, 2, 3, 4, 5, 1, 2, 3, 4)
    gathers = [
        Gather(buf, send.at[g], recv.at[g], level, at, SAME if g < 5 else MIXED, level < 4)
        for g, (buf, level) in enumerate(zip(bufs, groups))
    ]
    hs, ws, zs = gathers[:5], gathers[5:10], gathers[10:]

    def mine(gather):
        own = gather.own
        return (own["y"], own["z"], own["x"], core)

    loads = []

    def load(source, target):
        copy = pltpu.make_async_copy(source, target, load_sem.at[len(loads)])
        copy.start()
        loads.append(copy)

    load(dinv, d_v)
    load(off, l_v)
    load(rhs, b_v)
    row = 0
    for gather, held in zip(hs, HELD):
        load(front_rhs.at[pl.ds(row, held)], gather.buf.at[mine(gather)])
        row += held
    load(update, u_v)
    load(piv, m_v)
    load(factor, e_v)

    barrier = pltpu.get_barrier_semaphore()
    peers = [(at["y"], at["z"], (at["x"] + o) % 4, core) for o in (1, 2, 3)]
    peers += [
        ((at["y"] + oy) % 4, (at["z"] + oz) % 4, at["x"], core)
        for oy in range(4)
        for oz in range(4)
        if oy or oz
    ]
    peers.append((at["y"], at["z"], at["x"], 1 - core))
    for y, z, x, c in peers:
        pl.semaphore_signal(
            barrier, inc=1, device_id=(y * 4 + z, x * 2 + c), device_id_type=pl.DeviceIdType.MESH
        )
    pl.semaphore_wait(barrier, len(peers))

    for copy in loads[3:8]:
        copy.wait()
    both(lambda c: [gather.begin(c) for gather in hs])
    for copy in loads[:3]:
        copy.wait()
    loads[8].wait()

    def prepare(block, slot):
        high, low = split(d_v[block])
        wide = jnp.concatenate([l_v[block - 1, 0], l_v[block - 1, 1], b_v[block]], axis=1)
        wide_high, wide_low = split(wide)
        first = dot(jnp.concatenate([high, low], axis=0), wide_high)
        product = first[:B] + (first[B:] + dot(high, wide_low))
        g_v[slot] = stack(product[:, : 2 * B])
        c_v[slot] = product[:, 2 * B :]

    def keep(block, value):
        y_v[block] = value
        yhl_v[block] = side(value)

    def couple(block):
        columns = pl.ds(pl.multiple_of(block * B, B), B)
        acc_v[...] += fold(dot(stack(u_v[:, columns]), yhl_v[block]))

    keep(0, fold(dot(stack(d_v[0]), side(b_v[0]))))
    prepare(1, 1)
    acc_v[...] = jnp.zeros_like(acc_v)

    def advance(block, carry):
        slot = lax.rem(block, 2)
        known = jnp.concatenate([yhl_v[block - 1], yhl_v[table[COLUMNS_AT + block - 1, 0]]], axis=0)
        value = c_v[slot] - fold(dot(g_v[slot], known))
        couple(block - 1)
        prepare(jnp.minimum(block + 1, SB - 1), 1 - slot)
        keep(block, value)
        return carry

    lax.fori_loop(1, 17, advance, 0)
    both(lambda c: [gather.middle(c) for gather in hs])
    lax.fori_loop(17, SB, advance, 0)
    couple(SB - 1)

    stores = []

    def store(source, target):
        copy = pltpu.make_async_copy(source, target, store_sem.at[len(stores)])
        copy.start()
        stores.append(copy)

    def run(gather, before):
        both(gather.begin)
        before()

        def rest(c):
            gather.middle(c)
            gather.close(c)
            gather.finish(c)

        both(rest)

    def fill(level):
        gather = hs[level - 1]

        def rest(c):
            gather.close(c)
            gather.finish(c)

        both(rest)
        held = HELD[level - 1]
        many = 8 * held
        for y in range(YS[level - 1]):
            for z in range(ZS[level - 1]):
                first = (y * ZS[level - 1] + z) * many
                p_v[first : first + many, :] = gather.buf[y, z].reshape(many, N)

    w0_at = mine(ws[0])
    w0[w0_at] = -acc_v[...]

    def before_first():
        store(y_v, solved_out)
        fill(1)
        loads[9].wait()
        loads[10].wait()

    run(ws[0], before_first)

    def hit(entry, which):
        return table[entry, 8 + which].astype(F32)

    w0_blocks = w0.reshape(PB, B, N)

    def landed(entry):
        total = hit(entry, 0) * w0_blocks[table[entry, 0]]
        for s in range(1, 8):
            total = total + hit(entry, s) * w0_blocks[table[entry, s]]
        return total

    def place_first(block, carry):
        rows = pl.ds(pl.multiple_of(block * B, B), B)
        p_v[rows, :] = p_v[rows, :] + landed(block)
        return carry

    lax.fori_loop(0, PB, place_first, 0)

    def place(level):
        blocks = ws[level - 1].buf.reshape(2 * PB, B, N)

        def body(block, carry):
            rows = pl.ds(pl.multiple_of(block * B, B), B)
            entry = ENTRY_AT[level] + block
            total = p_v[rows, :]
            for child in (0, 1):
                total = total + hit(entry, child) * blocks[table[entry, child]]
            p_v[rows, :] = total
            return carry

        lax.fori_loop(0, PB, body, 0)

    def update_rows(level):
        if level == 1:
            return jnp.concatenate([landed(PB), landed(PB + 1)], axis=0)
        held = HELD[level - 1]
        pieces = ws[level - 1].buf.reshape(2 * ROWS // held, held, N)
        entry = ENTRY_AT[level] + PB
        return (
            hit(entry, 0) * pieces[table[entry, 0]] + hit(entry, 1) * pieces[table[entry, 1]]
        )

    def multiply(matrix, row, held, chunks):
        tall = min(held, B)
        totals = []
        for first in range(0, held, tall):
            total = None
            column = 0
            for right in chunks:
                depth = right.shape[0]
                left = stack(matrix[row + first : row + first + tall, column : column + depth])
                part = dot(left, right)
                total = part if total is None else total + part
                column += depth
            totals.append(fold(total))
        return totals[0] if len(totals) == 1 else jnp.concatenate(totals, axis=0)

    piv_row = 0
    upd_row = 0
    for level in range(1, LEVELS + 1):
        held = HELD[level - 1]
        value = multiply(m_v, piv_row, held, [side(p_v[...])])
        if level == LEVELS:
            last_v[...] = value
            store(last_v, front_out.at[pl.ds(piv_row, held)])
            break
        gather = zs[level - 1]
        at_own = mine(gather)
        gather.buf[at_own] = value

        def before_solution(level=level, gather=gather, row=piv_row, held=held):
            store(gather.buf.at[mine(gather)], front_out.at[pl.ds(row, held)])
            fill(level + 1)

        run(gather, before_solution)
        chunks = [
            side(gather.buf[y, z].reshape(8 * held, N))
            for y in range(YS[level - 1])
            for z in range(ZS[level - 1])
        ]
        below = update_rows(level) - multiply(e_v, upd_row, held, chunks)
        wide = ws[level]
        wide_at = mine(wide)
        wide.buf[wide_at] = below
        run(wide, lambda: None)
        place(level + 1)
        piv_row += held
        upd_row += held

    both(lambda c: [gather.drain(c) for gather in gathers])
    for copy in stores:
        copy.wait()


def tables(sub_pattern, sub_map, front_map):
    leaf = lax.axis_index("leaf")
    front = lax.axis_index("front")
    pivots = jnp.arange(PB, dtype=jnp.int32)
    places, flags = [], []
    maps = lax.dynamic_slice_in_dim(sub_map, leaf * 8, 8)
    wanted = jnp.concatenate([pivots, PB + 2 * front + jnp.arange(2, dtype=jnp.int32)])
    match = maps[None] == wanted[:, None, None]
    places.append(2 * jnp.arange(8, dtype=jnp.int32) + match[:, :, 1].astype(jnp.int32))
    flags.append(match.any(axis=2))
    for level in range(2, LEVELS + 1):
        held = HELD[level - 1]
        maps = lax.dynamic_slice_in_dim(
            front_map, MAP_AT[level - 2] + 2 * (leaf // 2 ** (level - 1)), 2
        )
        row = ((leaf % 2 ** (level - 1)) * 8 + front) * held
        wanted = jnp.concatenate([pivots, (PB + row // B)[None]])
        match = maps[None] == wanted[:, None, None]
        place = jnp.sum(match * jnp.arange(PB, dtype=jnp.int32), axis=2, dtype=jnp.int32)
        place = place + jnp.array([0, PB], jnp.int32)
        last = jnp.arange(PB + 1)[:, None] == PB
        place = jnp.where(last, place * (B // held) + row % B // held, place)
        places.append(jnp.pad(place, ((0, 0), (0, 6))))
        flags.append(jnp.pad(match.any(axis=2), ((0, 0), (0, 6))))
    found = jnp.concatenate([jnp.concatenate(places), jnp.concatenate(flags).astype(jnp.int32)], axis=1)
    return jnp.concatenate([found, jnp.pad(sub_pattern[:, 1:], ((0, 0), (0, 15)))])


def per_device(
    sub_rhs, sub_dinv, sub_off, sub_pattern, sub_update, sub_map,
    front_rhs, piv_inverse, upd_factor, front_map,
):
    def wide(level, held):
        return pltpu.VMEM((YS[level - 1], ZS[level - 1], 4, 2, held, N), F32)

    scratch = [
        pltpu.VMEM((SB, B, N), F32),
        pltpu.VMEM((SB, B, B), F32),
        pltpu.VMEM((SB - 1, K, B, B), F32),
        pltpu.VMEM((2 * B, SB * B), F32),
        pltpu.VMEM((PROWS, ROWS), F32),
        pltpu.VMEM((UROWS, ROWS), F32),
        pltpu.VMEM((SB, B, N), F32),
        pltpu.VMEM((SB, B, 2 * N), BF16),
        pltpu.VMEM((2, 2 * B, 2 * B), BF16),
        pltpu.VMEM((2, B, N), F32),
        pltpu.VMEM((2 * B, N), F32),
        pltpu.VMEM((ROWS, N), F32),
        pltpu.VMEM((HELD[-1], N), F32),
    ]
    scratch += [wide(level, HELD[level - 1]) for level in range(1, 6)]
    scratch += [wide(1, 256)]
    scratch += [wide(level + 1, HELD[level - 1]) for level in range(1, 5)]
    scratch += [wide(level, HELD[level - 1]) for level in range(1, 5)]
    scratch += [
        pltpu.SemaphoreType.DMA((11,)),
        pltpu.SemaphoreType.DMA((6,)),
        pltpu.SemaphoreType.DMA((14, COPIES)),
        pltpu.SemaphoreType.DMA((14, COPIES)),
    ]
    smem = pl.BlockSpec(memory_space=pltpu.SMEM)
    hbm = pl.BlockSpec(memory_space=pl.ANY)
    solved, fronts = pl.pallas_call(
        kernel,
        out_shape=(
            jax.ShapeDtypeStruct((SB, B, N), F32),
            jax.ShapeDtypeStruct((PROWS, N), F32),
        ),
        in_specs=[smem] + [hbm] * 7,
        out_specs=(hbm, hbm),
        scratch_shapes=scratch,
        compiler_params=pltpu.CompilerParams(
            collective_id=0, has_side_effects=True, vmem_limit_bytes=62 * 2**20
        ),
    )(
        tables(sub_pattern, sub_map, front_map),
        sub_rhs.reshape(SB, B, N), sub_dinv, sub_off, sub_update, front_rhs, piv_inverse, upd_factor,
    )
    return solved.reshape(SB * B, N), fronts


def solution(mesh):
    rows = P(("leaf", "front"), None)
    return jax.shard_map(
        per_device,
        mesh=mesh,
        in_specs=(
            rows,
            P(("leaf", "front"), None, None),
            P(("leaf", "front"), None, None, None),
            rows,
            rows,
            P(),
            rows,
            rows,
            rows,
            P(),
        ),
        out_specs=(rows, rows),
        check_vma=False,
    )
```

```python
import itertools

import jax
import jax.numpy as jnp
from jax import lax
from jax.experimental import pallas as pl
from jax.experimental.pallas import tpu as pltpu
from jax.sharding import PartitionSpec as P

B = 128
N = 128
SB = 24
K = 2
ROWS = 2048
PB = 16
LEVELS = 5
PROWS = 496
UROWS = 480
MAPROWS = 30
YS = (1, 1, 1, 2, 4)
ZS = (1, 2, 4, 4, 4)
HELD = (256, 128, 64, 32, 16)
MAP_AT = (0, 16, 24, 28)
ENTRY_AT = (None, 0, 18, 35, 52, 69)
MIXED = (("x", "zy"), ("zy", "x"))
SAME = (("x", "zy"), ("x", "zy"))
CROSS = 18
COPIES = CROSS + 19
COLUMNS_AT = 86
EARLY = 8
F32 = jnp.float32
BF16 = jnp.bfloat16


def split(value):
    high = value.astype(BF16)
    return high, (value - high.astype(F32)).astype(BF16)


def side(value):
    return jnp.concatenate(split(value), axis=1)


def stack(value):
    return jnp.concatenate(split(value), axis=0)


def dot(left, right):
    return jnp.dot(left, right, preferred_element_type=F32)


def fold(product):
    half = product.shape[0] // 2
    return product[:half, :N] + (product[:half, N:] + product[half:, :N])


class Gather:
    def __init__(self, buf, send, recv, level, at, order, eager):
        self.buf, self.send, self.recv, self.at = buf, send, recv, at
        self.size = {"x": 4, "z": ZS[level - 1], "y": YS[level - 1]}
        self.order, self.eager = order, eager
        self.own = {d: 0 if self.size[d] == 1 else at[d] % self.size[d] for d in "yzx"}

    def sets(self, core):
        found = ["".join(d for d in dims if self.size[d] > 1) for dims in self.order[core]]
        return found[0] or found[1], found[1] if found[0] else ""

    def hops(self, dims):
        steps = [
            dict(zip(dims, offsets))
            for offsets in itertools.product(*(range(self.size[d]) for d in dims))
            if any(offsets)
        ]
        return sorted(steps, key=lambda step: sum(min(o, self.size[d] - o) for d, o in step.items()))

    def moved(self, dim, offset):
        here = self.at[dim]
        if offset == 0:
            return here
        if self.size[dim] == 4:
            return (here + offset) % 4
        return here + 1 - 2 * (here % 2)

    def origin(self, step):
        return {
            d: self.moved(d, -o % self.size[d]) % self.size[d] for d, o in step.items()
        }

    def view(self, core, full="", **places):
        place = {**self.own, **places}
        index = [slice(None) if d in full else place[d] for d in "yzx"]
        return self.buf.at[index[0], index[1], index[2], core]

    def copy(self, view, which, **changes):
        place = {**self.at, **changes}
        return pltpu.make_async_remote_copy(
            src_ref=view,
            dst_ref=view,
            send_sem=self.send.at[which],
            recv_sem=self.recv.at[which],
            device_id=(place["y"] * 4 + place["z"], place["x"] * 2 + place["core"]),
            device_id_type=pl.DeviceIdType.MESH,
        )

    def to(self, step):
        return {d: self.moved(d, o) for d, o in step.items()}

    def out(self, view, which, core, step):
        return lambda: self.copy(view, which, core=core, **self.to(step))

    def across(self, view, which, core):
        return lambda: self.copy(view, which, core=1 - core)

    def plan(self, core):
        first, second = self.sets(core)
        near, far = self.hops(first), self.hops(second) if second else []
        cross = CROSS
        begin = [self.out(self.view(core), i, core, step) for i, step in enumerate(near)]
        used = len(near)
        mine = [(self.view(core), cross)]
        middle, close = [], []
        held = [{}] + [self.origin(step) for step in near]
        sets = [held[i : i + 1] for i in range(len(held))] if self.eager else [held]
        sends = []
        for group in sets:
            view = self.view(core, **group[0]) if self.eager else self.view(core, first)
            sends.append([self.out(view, used + j, core, step) for j, step in enumerate(far)])
            used += len(far)
        if self.eager:
            begin += sends[0]
        for i, step in enumerate(near):
            view = self.view(core, **held[i + 1])
            mine.append((view, cross + 1 + i))
            after = sends[i + 1] if self.eager else sends[0] if i == len(near) - 1 else []
            middle.append(([(view, i)], after + [self.across(view, cross + 1 + i, core)]))
        if not second:
            middle = [(wait, [start[-1]]) for wait, start in middle]
        for j, step in enumerate(far):
            origin = self.origin(step)
            waits = []
            for g, group in enumerate(sets):
                if self.eager:
                    view = self.view(core, **{**group[0], **origin})
                else:
                    view = self.view(core, first, **origin)
                waits.append((view, len(near) + g * len(far) + j))
            view, which = self.view(core, first, **origin), cross + 1 + len(near) + j
            mine.append((view, which))
            close.append((waits, [self.across(view, which, core)]))
        begin.append(self.across(self.view(core), cross, core))
        return begin, middle, close, mine

    def begin(self, core):
        for make in self.plan(core)[0]:
            make().start()

    def follow(self, steps, core):
        for waits, starts in steps:
            for view, which in waits:
                self.copy(view, which, core=1 - core).wait_recv()
            for make in starts:
                make().start()

    def middle(self, core):
        self.follow(self.plan(core)[1], core)

    def close(self, core):
        self.follow(self.plan(core)[2], core)

    def finish(self, core):
        for view, which in self.plan(1 - core)[3]:
            self.copy(view, which, core=1 - core).wait_recv()

    def drain(self, core):
        begin, middle, close, _ = self.plan(core)
        for make in begin + [make for _, starts in middle + close for make in starts]:
            make().wait_send()


def kernel(
    table,
    rhs, dinv, off, update, front_rhs, piv, factor,
    solved_out, front_out,
    b_v, d_v, l_v, u_v, m_v, e_v, y_v, yhl_v, g_v, c_v, acc_v, p_v, last_v,
    h1, h2, h3, h4, h5, w0, w1, w2, w3, w4, z1, z2, z3, z4,
    load_sem, store_sem, send, recv,
):
    leaf = lax.axis_index("leaf")
    front = lax.axis_index("front")
    core = front % 2
    at = {"y": leaf // 4, "z": leaf % 4, "x": front // 2, "core": core}

    def both(step):
        for which in (0, 1):
            @pl.when(core == which)
            def _():
                step(which)

    bufs = (h1, h2, h3, h4, h5, w0, w1, w2, w3, w4, z1, z2, z3, z4)
    groups = (1, 2, 3, 4, 5, 1, 2, 3, 4, 5, 1, 2, 3, 4)
    gathers = [
        Gather(buf, send.at[g], recv.at[g], level, at, SAME if g < 5 else MIXED, level < 4)
        for g, (buf, level) in enumerate(zip(bufs, groups))
    ]
    hs, ws, zs = gathers[:5], gathers[5:10], gathers[10:]

    def mine(gather):
        own = gather.own
        return (own["y"], own["z"], own["x"], core)

    loads = []

    def load(source, target):
        copy = pltpu.make_async_copy(source, target, load_sem.at[len(loads)])
        copy.start()
        loads.append(copy)

    row = 0
    for gather, held in zip(hs, HELD):
        load(front_rhs.at[pl.ds(row, held)], gather.buf.at[mine(gather)])
        row += held
    for first, many in ((0, EARLY), (EARLY, SB - EARLY)):
        load(dinv.at[pl.ds(first, many)], d_v.at[pl.ds(first, many)])
        load(off.at[pl.ds(first, many - first // EARLY)], l_v.at[pl.ds(first, many - first // EARLY)])
        load(rhs.at[pl.ds(first, many)], b_v.at[pl.ds(first, many)])
        columns = pl.ds(first * B, many * B)
        load(update.at[:, columns], u_v.at[:, columns])
    load(piv, m_v)
    load(factor, e_v)

    barrier = pltpu.get_barrier_semaphore()
    peers = [(at["y"], at["z"], (at["x"] + o) % 4, core) for o in (1, 2, 3)]
    peers += [
        ((at["y"] + oy) % 4, (at["z"] + oz) % 4, at["x"], core)
        for oy in range(4)
        for oz in range(4)
        if oy or oz
    ]
    peers.append((at["y"], at["z"], at["x"], 1 - core))
    for y, z, x, c in peers:
        pl.semaphore_signal(
            barrier, inc=1, device_id=(y * 4 + z, x * 2 + c), device_id_type=pl.DeviceIdType.MESH
        )
    pl.semaphore_wait(barrier, len(peers))

    for copy in loads[:5]:
        copy.wait()
    both(lambda c: [gather.begin(c) for gather in hs])
    for copy in loads[5:9]:
        copy.wait()

    def prepare(block, slot):
        high, low = split(d_v[block])
        wide = jnp.concatenate([l_v[block - 1, 0], l_v[block - 1, 1], b_v[block]], axis=1)
        wide_high, wide_low = split(wide)
        first = dot(jnp.concatenate([high, low], axis=0), wide_high)
        product = first[:B] + (first[B:] + dot(high, wide_low))
        g_v[slot] = stack(product[:, : 2 * B])
        c_v[slot] = product[:, 2 * B :]

    def keep(block, value):
        y_v[block] = value
        yhl_v[block] = side(value)

    def couple(block):
        columns = pl.ds(pl.multiple_of(block * B, B), B)
        acc_v[...] += fold(dot(stack(u_v[:, columns]), yhl_v[block]))

    keep(0, fold(dot(stack(d_v[0]), side(b_v[0]))))
    prepare(1, 1)
    acc_v[...] = jnp.zeros_like(acc_v)

    def advance(block, carry):
        slot = lax.rem(block, 2)
        known = jnp.concatenate([yhl_v[block - 1], yhl_v[table[COLUMNS_AT + block - 1, 0]]], axis=0)
        value = c_v[slot] - fold(dot(g_v[slot], known))
        couple(block - 1)
        prepare(jnp.minimum(block + 1, SB - 1), 1 - slot)
        keep(block, value)
        return carry

    lax.fori_loop(1, EARLY - 1, advance, 0)
    for copy in loads[9:13]:
        copy.wait()
    lax.fori_loop(EARLY - 1, SB, advance, 0)
    couple(SB - 1)

    stores = []

    def store(source, target):
        copy = pltpu.make_async_copy(source, target, store_sem.at[len(stores)])
        copy.start()
        stores.append(copy)

    def run(gather, before):
        both(gather.begin)
        before()

        def rest(c):
            gather.middle(c)
            gather.close(c)
            gather.finish(c)

        both(rest)

    def fill(level):
        gather = hs[level - 1]

        def rest(c):
            gather.close(c)
            gather.finish(c)

        both(rest)
        held = HELD[level - 1]
        many = 8 * held
        for y in range(YS[level - 1]):
            for z in range(ZS[level - 1]):
                first = (y * ZS[level - 1] + z) * many
                p_v[first : first + many, :] = gather.buf[y, z].reshape(many, N)

    w0_at = mine(ws[0])
    w0[w0_at] = -acc_v[...]

    def before_first():
        both(lambda c: [gather.middle(c) for gather in hs])
        store(y_v, solved_out)
        fill(1)
        loads[13].wait()
        loads[14].wait()

    run(ws[0], before_first)

    def hit(entry, which):
        return table[entry, 8 + which].astype(F32)

    w0_blocks = w0.reshape(PB, B, N)

    def landed(entry):
        total = hit(entry, 0) * w0_blocks[table[entry, 0]]
        for s in range(1, 8):
            total = total + hit(entry, s) * w0_blocks[table[entry, s]]
        return total

    def place_first(block, carry):
        rows = pl.ds(pl.multiple_of(block * B, B), B)
        p_v[rows, :] = p_v[rows, :] + landed(block)
        return carry

    lax.fori_loop(0, PB, place_first, 0)

    def place(level):
        blocks = ws[level - 1].buf.reshape(2 * PB, B, N)

        def body(block, carry):
            rows = pl.ds(pl.multiple_of(block * B, B), B)
            entry = ENTRY_AT[level] + block
            total = p_v[rows, :]
            for child in (0, 1):
                total = total + hit(entry, child) * blocks[table[entry, child]]
            p_v[rows, :] = total
            return carry

        lax.fori_loop(0, PB, body, 0)

    def update_rows(level):
        if level == 1:
            return jnp.concatenate([landed(PB), landed(PB + 1)], axis=0)
        held = HELD[level - 1]
        pieces = ws[level - 1].buf.reshape(2 * ROWS // held, held, N)
        entry = ENTRY_AT[level] + PB
        return (
            hit(entry, 0) * pieces[table[entry, 0]] + hit(entry, 1) * pieces[table[entry, 1]]
        )

    def multiply(matrix, row, held, chunks):
        tall = min(held, B)
        totals = []
        for first in range(0, held, tall):
            total = None
            column = 0
            for right in chunks:
                depth = right.shape[0]
                left = stack(matrix[row + first : row + first + tall, column : column + depth])
                part = dot(left, right)
                total = part if total is None else total + part
                column += depth
            totals.append(fold(total))
        return totals[0] if len(totals) == 1 else jnp.concatenate(totals, axis=0)

    piv_row = 0
    upd_row = 0
    for level in range(1, LEVELS + 1):
        held = HELD[level - 1]
        value = multiply(m_v, piv_row, held, [side(p_v[...])])
        if level == LEVELS:
            last_v[...] = value
            store(last_v, front_out.at[pl.ds(piv_row, held)])
            break
        gather = zs[level - 1]
        at_own = mine(gather)
        gather.buf[at_own] = value

        def before_solution(level=level, gather=gather, row=piv_row, held=held):
            store(gather.buf.at[mine(gather)], front_out.at[pl.ds(row, held)])
            fill(level + 1)

        run(gather, before_solution)
        chunks = [
            side(gather.buf[y, z].reshape(8 * held, N))
            for y in range(YS[level - 1])
            for z in range(ZS[level - 1])
        ]
        below = update_rows(level) - multiply(e_v, upd_row, held, chunks)
        wide = ws[level]
        wide_at = mine(wide)
        wide.buf[wide_at] = below
        run(wide, lambda: None)
        place(level + 1)
        piv_row += held
        upd_row += held

    both(lambda c: [gather.drain(c) for gather in gathers])
    for copy in stores:
        copy.wait()


def tables(sub_pattern, sub_map, front_map):
    leaf = lax.axis_index("leaf")
    front = lax.axis_index("front")
    pivots = jnp.arange(PB, dtype=jnp.int32)
    places, flags = [], []
    maps = lax.dynamic_slice_in_dim(sub_map, leaf * 8, 8)
    wanted = jnp.concatenate([pivots, PB + 2 * front + jnp.arange(2, dtype=jnp.int32)])
    match = maps[None] == wanted[:, None, None]
    places.append(2 * jnp.arange(8, dtype=jnp.int32) + match[:, :, 1].astype(jnp.int32))
    flags.append(match.any(axis=2))
    for level in range(2, LEVELS + 1):
        held = HELD[level - 1]
        maps = lax.dynamic_slice_in_dim(
            front_map, MAP_AT[level - 2] + 2 * (leaf // 2 ** (level - 1)), 2
        )
        row = ((leaf % 2 ** (level - 1)) * 8 + front) * held
        wanted = jnp.concatenate([pivots, (PB + row // B)[None]])
        match = maps[None] == wanted[:, None, None]
        place = jnp.sum(match * jnp.arange(PB, dtype=jnp.int32), axis=2, dtype=jnp.int32)
        place = place + jnp.array([0, PB], jnp.int32)
        last = jnp.arange(PB + 1)[:, None] == PB
        place = jnp.where(last, place * (B // held) + row % B // held, place)
        places.append(jnp.pad(place, ((0, 0), (0, 6))))
        flags.append(jnp.pad(match.any(axis=2), ((0, 0), (0, 6))))
    found = jnp.concatenate([jnp.concatenate(places), jnp.concatenate(flags).astype(jnp.int32)], axis=1)
    return jnp.concatenate([found, jnp.pad(sub_pattern[:, 1:], ((0, 0), (0, 15)))])


def per_device(
    sub_rhs, sub_dinv, sub_off, sub_pattern, sub_update, sub_map,
    front_rhs, piv_inverse, upd_factor, front_map,
):
    def wide(level, held):
        return pltpu.VMEM((YS[level - 1], ZS[level - 1], 4, 2, held, N), F32)

    scratch = [
        pltpu.VMEM((SB, B, N), F32),
        pltpu.VMEM((SB, B, B), F32),
        pltpu.VMEM((SB - 1, K, B, B), F32),
        pltpu.VMEM((2 * B, SB * B), F32),
        pltpu.VMEM((PROWS, ROWS), F32),
        pltpu.VMEM((UROWS, ROWS), F32),
        pltpu.VMEM((SB, B, N), F32),
        pltpu.VMEM((SB, B, 2 * N), BF16),
        pltpu.VMEM((2, 2 * B, 2 * B), BF16),
        pltpu.VMEM((2, B, N), F32),
        pltpu.VMEM((2 * B, N), F32),
        pltpu.VMEM((ROWS, N), F32),
        pltpu.VMEM((HELD[-1], N), F32),
    ]
    scratch += [wide(level, HELD[level - 1]) for level in range(1, 6)]
    scratch += [wide(1, 256)]
    scratch += [wide(level + 1, HELD[level - 1]) for level in range(1, 5)]
    scratch += [wide(level, HELD[level - 1]) for level in range(1, 5)]
    scratch += [
        pltpu.SemaphoreType.DMA((15,)),
        pltpu.SemaphoreType.DMA((6,)),
        pltpu.SemaphoreType.DMA((14, COPIES)),
        pltpu.SemaphoreType.DMA((14, COPIES)),
    ]
    smem = pl.BlockSpec(memory_space=pltpu.SMEM)
    hbm = pl.BlockSpec(memory_space=pl.ANY)
    solved, fronts = pl.pallas_call(
        kernel,
        out_shape=(
            jax.ShapeDtypeStruct((SB, B, N), F32),
            jax.ShapeDtypeStruct((PROWS, N), F32),
        ),
        in_specs=[smem] + [hbm] * 7,
        out_specs=(hbm, hbm),
        scratch_shapes=scratch,
        compiler_params=pltpu.CompilerParams(
            collective_id=0, has_side_effects=True, vmem_limit_bytes=62 * 2**20
        ),
    )(
        tables(sub_pattern, sub_map, front_map),
        sub_rhs.reshape(SB, B, N), sub_dinv, sub_off, sub_update, front_rhs, piv_inverse, upd_factor,
    )
    return solved.reshape(SB * B, N), fronts


def solution(mesh):
    rows = P(("leaf", "front"), None)
    return jax.shard_map(
        per_device,
        mesh=mesh,
        in_specs=(
            rows,
            P(("leaf", "front"), None, None),
            P(("leaf", "front"), None, None, None),
            rows,
            rows,
            P(),
            rows,
            rows,
            rows,
            P(),
        ),
        out_specs=(rows, rows),
        check_vma=False,
    )
```

```python
import itertools

import jax
import jax.numpy as jnp
from jax import lax
from jax.experimental import pallas as pl
from jax.experimental.pallas import tpu as pltpu
from jax.sharding import PartitionSpec as P

B = 128
N = 128
SB = 24
K = 2
ROWS = 2048
PB = 16
LEVELS = 5
PROWS = 496
UROWS = 480
MAPROWS = 30
YS = (1, 1, 1, 2, 4)
ZS = (1, 2, 4, 4, 4)
HELD = (256, 128, 64, 32, 16)
MAP_AT = (0, 16, 24, 28)
ENTRY_AT = (None, 0, 18, 35, 52, 69)
MIXED = (("x", "zy"), ("zy", "x"))
SAME = (("x", "zy"), ("x", "zy"))
SENDS = (3, 7, 15, 10, 18)
COPIES = (7, 12, 22, 21, 37)
HALF = 64
COLUMNS_AT = 86
EARLY = 8
F32 = jnp.float32
BF16 = jnp.bfloat16


def split(value):
    high = value.astype(BF16)
    return high, (value - high.astype(F32)).astype(BF16)


def side(value):
    return jnp.concatenate(split(value), axis=1)


def stack(value):
    return jnp.concatenate(split(value), axis=0)


def dot(left, right):
    return jnp.dot(left, right, preferred_element_type=F32)


def fold(product):
    half = product.shape[0] // 2
    return product[:half, :N] + (product[:half, N:] + product[half:, :N])


def low_half(shape):
    return lax.broadcasted_iota(jnp.int32, shape, len(shape) - 1) < HALF


def turned(value):
    return pltpu.roll(value, HALF, 1)


def merged(left, right):
    return jnp.where(low_half(left.shape), left, turned(right))


def pack(value):
    rows = value.shape[0]
    unit = min(rows, B)
    parts = []
    for first in range(0, rows, unit):
        middle = first + unit // 2
        parts.append(merged(value[first:middle], value[middle : first + unit]))
    return parts[0] if len(parts) == 1 else jnp.concatenate(parts, axis=0)


def unpack(value, unit):
    rows = value.shape[0]
    shape = (2 * rows // unit, unit // 2, N)
    pair = jnp.concatenate([value.reshape(shape), turned(value).reshape(shape)], axis=1)
    return pair.reshape(2 * rows, N)


def narrow(value):
    high = value.astype(BF16).astype(F32)
    return merged(high, value - high).astype(BF16)


def fold_narrow(product):
    half = product.shape[0] // 2
    top = product[:half]
    return top + (turned(top) + product[half:])


class Gather:
    def __init__(self, buf, send, recv, base, level, at, order):
        self.buf, self.send, self.recv, self.at = buf, send, recv, at
        self.base, self.level, eager = base, level, level < 4
        self.size = {"x": 4, "z": ZS[level - 1], "y": YS[level - 1]}
        self.order, self.eager = order, eager
        self.own = {d: 0 if self.size[d] == 1 else at[d] % self.size[d] for d in "yzx"}

    def sets(self, core):
        found = ["".join(d for d in dims if self.size[d] > 1) for dims in self.order[core]]
        return found[0] or found[1], found[1] if found[0] else ""

    def hops(self, dims):
        steps = [
            dict(zip(dims, offsets))
            for offsets in itertools.product(*(range(self.size[d]) for d in dims))
            if any(offsets)
        ]
        return sorted(steps, key=lambda step: sum(min(o, self.size[d] - o) for d, o in step.items()))

    def moved(self, dim, offset):
        here = self.at[dim]
        if offset == 0:
            return here
        if self.size[dim] == 4:
            return (here + offset) % 4
        return here + 1 - 2 * (here % 2)

    def origin(self, step):
        return {
            d: self.moved(d, -o % self.size[d]) % self.size[d] for d, o in step.items()
        }

    def view(self, core, full="", **places):
        place = {**self.own, **places}
        index = [slice(None) if d in full else place[d] for d in "yzx"]
        return self.buf.at[index[0], index[1], index[2], core]

    def copy(self, view, which, **changes):
        place = {**self.at, **changes}
        return pltpu.make_async_remote_copy(
            src_ref=view,
            dst_ref=view,
            send_sem=self.send.at[self.base + which],
            recv_sem=self.recv.at[self.base + which],
            device_id=(place["y"] * 4 + place["z"], place["x"] * 2 + place["core"]),
            device_id_type=pl.DeviceIdType.MESH,
        )

    def to(self, step):
        return {d: self.moved(d, o) for d, o in step.items()}

    def out(self, view, which, core, step):
        return lambda: self.copy(view, which, core=core, **self.to(step))

    def across(self, view, which, core):
        return lambda: self.copy(view, which, core=1 - core)

    def plan(self, core):
        first, second = self.sets(core)
        near, far = self.hops(first), self.hops(second) if second else []
        cross = SENDS[self.level - 1]
        begin = [self.out(self.view(core), i, core, step) for i, step in enumerate(near)]
        used = len(near)
        mine = [(self.view(core), cross)]
        middle, close = [], []
        held = [{}] + [self.origin(step) for step in near]
        sets = [held[i : i + 1] for i in range(len(held))] if self.eager else [held]
        sends = []
        for group in sets:
            view = self.view(core, **group[0]) if self.eager else self.view(core, first)
            sends.append([self.out(view, used + j, core, step) for j, step in enumerate(far)])
            used += len(far)
        if self.eager:
            begin += sends[0]
        for i, step in enumerate(near):
            view = self.view(core, **held[i + 1])
            mine.append((view, cross + 1 + i))
            after = sends[i + 1] if self.eager else sends[0] if i == len(near) - 1 else []
            middle.append(([(view, i)], after + [self.across(view, cross + 1 + i, core)]))
        if not second:
            middle = [(wait, [start[-1]]) for wait, start in middle]
        for j, step in enumerate(far):
            origin = self.origin(step)
            waits = []
            for g, group in enumerate(sets):
                if self.eager:
                    view = self.view(core, **{**group[0], **origin})
                else:
                    view = self.view(core, first, **origin)
                waits.append((view, len(near) + g * len(far) + j))
            view, which = self.view(core, first, **origin), cross + 1 + len(near) + j
            mine.append((view, which))
            close.append((waits, [self.across(view, which, core)]))
        begin.append(self.across(self.view(core), cross, core))
        return begin, middle, close, mine

    def begin(self, core):
        for make in self.plan(core)[0]:
            make().start()

    def follow(self, steps, core):
        for waits, starts in steps:
            for view, which in waits:
                self.copy(view, which, core=1 - core).wait_recv()
            for make in starts:
                make().start()

    def middle(self, core):
        self.follow(self.plan(core)[1], core)

    def close(self, core):
        self.follow(self.plan(core)[2], core)

    def finish(self, core):
        for view, which in self.plan(1 - core)[3]:
            self.copy(view, which, core=1 - core).wait_recv()

    def drain(self, core):
        begin, middle, close, _ = self.plan(core)
        for make in begin + [make for _, starts in middle + close for make in starts]:
            make().wait_send()


def kernel(
    table,
    rhs, dinv, off, update, front_rhs, piv, factor,
    solved_out, front_out,
    b_v, d_v, l_v, u_v, m_v, e_v, y_v, yhl_v, g_v, c_v, acc_v, p_v, ms_v, es_v, z_v,
    h1, h2, h3, h4, h5, *rest,
):
    leaf = lax.axis_index("leaf")
    front = lax.axis_index("front")
    core = front % 2
    at = {"y": leaf // 4, "z": leaf % 4, "x": front // 2, "core": core}

    def both(step):
        for which in (0, 1):
            @pl.when(core == which)
            def _():
                step(which)

    streams, (load_sem, store_sem, send, recv) = rest[:18], rest[18:]
    levels = [1, 2, 3, 4, 5] + 2 * [1, 2, 3, 4, 5, 1, 2, 3, 4]
    gathers = []
    base = 0
    for buf, level in zip((h1, h2, h3, h4, h5, *streams), levels):
        order = SAME if len(gathers) < 5 else MIXED
        gathers.append(Gather(buf, send, recv, base, level, at, order))
        base += COPIES[level - 1]
    hs = gathers[:5]
    ws = (gathers[5:10], gathers[14:19])
    zs = (gathers[10:14], gathers[19:23])

    def mine(gather):
        own = gather.own
        return (own["y"], own["z"], own["x"], core)

    loads = []

    def load(source, target):
        copy = pltpu.make_async_copy(source, target, load_sem.at[len(loads)])
        copy.start()
        loads.append(copy)

    row = 0
    for gather, held in zip(hs, HELD):
        load(front_rhs.at[pl.ds(row, held)], gather.buf.at[mine(gather)])
        row += held
    for first, many in ((0, EARLY), (EARLY, SB - EARLY)):
        load(dinv.at[pl.ds(first, many)], d_v.at[pl.ds(first, many)])
        load(off.at[pl.ds(first, many - first // EARLY)], l_v.at[pl.ds(first, many - first // EARLY)])
        load(rhs.at[pl.ds(first, many)], b_v.at[pl.ds(first, many)])
        columns = pl.ds(first * B, many * B)
        load(update.at[:, columns], u_v.at[:, columns])
    load(piv, m_v)
    load(factor, e_v)

    barrier = pltpu.get_barrier_semaphore()
    peers = [(at["y"], at["z"], (at["x"] + o) % 4, core) for o in (1, 2, 3)]
    peers += [
        ((at["y"] + oy) % 4, (at["z"] + oz) % 4, at["x"], core)
        for oy in range(4)
        for oz in range(4)
        if oy or oz
    ]
    peers.append((at["y"], at["z"], at["x"], 1 - core))
    for y, z, x, c in peers:
        pl.semaphore_signal(
            barrier, inc=1, device_id=(y * 4 + z, x * 2 + c), device_id_type=pl.DeviceIdType.MESH
        )
    pl.semaphore_wait(barrier, len(peers))

    for copy in loads[:5]:
        copy.wait()
    both(lambda c: [gather.begin(c) for gather in hs])
    for copy in loads[5:9]:
        copy.wait()

    def prepare(block, slot):
        high, low = split(d_v[block])
        wide = jnp.concatenate([l_v[block - 1, 0], l_v[block - 1, 1], b_v[block]], axis=1)
        wide_high, wide_low = split(wide)
        first = dot(jnp.concatenate([high, low], axis=0), wide_high)
        product = first[:B] + (first[B:] + dot(high, wide_low))
        g_v[slot] = stack(product[:, : 2 * B])
        c_v[slot] = product[:, 2 * B :]

    def keep(block, value):
        y_v[block] = value
        yhl_v[block] = side(value)

    def couple(block):
        columns = pl.ds(pl.multiple_of(block * B, B), B)
        acc_v[...] += fold(dot(stack(u_v[:, columns]), yhl_v[block]))

    keep(0, fold(dot(stack(d_v[0]), side(b_v[0]))))
    prepare(1, 1)
    acc_v[...] = jnp.zeros_like(acc_v)

    def advance(block, carry):
        slot = lax.rem(block, 2)
        known = jnp.concatenate([yhl_v[block - 1], yhl_v[table[COLUMNS_AT + block - 1, 0]]], axis=0)
        value = c_v[slot] - fold(dot(g_v[slot], known))
        couple(block - 1)
        prepare(jnp.minimum(block + 1, SB - 1), 1 - slot)
        keep(block, value)
        return carry

    lax.fori_loop(1, EARLY - 1, advance, 0)
    for copy in loads[9:13]:
        copy.wait()
    lax.fori_loop(EARLY - 1, SB, advance, 0)
    couple(SB - 1)

    stores = []

    def store(source, target):
        copy = pltpu.make_async_copy(source, target, store_sem.at[len(stores)])
        copy.start()
        stores.append(copy)

    def widen(source, target, level, row, held):
        tall = min(held, B)
        for first in range(row, row + held, tall):
            target[2 * first : 2 * (first + tall), :] = stack(source[first : first + tall, :])

    def fill(level):
        gather = hs[level - 1]

        def rest(c):
            gather.close(c)
            gather.finish(c)

        both(rest)
        held = HELD[level - 1]
        many = 8 * held
        for y in range(YS[level - 1]):
            for z in range(ZS[level - 1]):
                first = (y * ZS[level - 1] + z) * many
                part = gather.buf[y, z].reshape(many, N)
                p_v[0, first : first + many, :] = part
                p_v[1, first : first + many, :] = turned(part)

    def send_update(stream, level, value):
        gather = ws[stream][level]
        own = mine(gather)
        gather.buf[own] = pack(value)
        both(gather.begin)

    def hit(entry, which):
        return table[entry, 8 + which].astype(F32)

    def landed(stream, level, entry):
        gather = ws[stream][level - 1]
        blocks = gather.buf.reshape(PB if level == 1 else 2 * PB, HALF, N)
        total = hit(entry, 0) * blocks[table[entry, 0]]
        for child in range(1, 8 if level == 1 else 2):
            total = total + hit(entry, child) * blocks[table[entry, child]]
        return total

    def place(stream, level):
        unit = B if level == 1 else min(B, HELD[level - 2])

        def body(block, carry):
            rows = pl.ds(pl.multiple_of(block * B, B), B)
            total = unpack(landed(stream, level, ENTRY_AT[level] + block), unit)
            p_v[stream, rows, :] = p_v[stream, rows, :] + total
            return carry

        lax.fori_loop(0, PB, body, 0)

    def update_rows(stream, level):
        entry = ENTRY_AT[level] + PB
        if level == 1:
            parts = [unpack(landed(stream, 1, entry + i), B) for i in (0, 1)]
            return jnp.concatenate(parts, axis=0)
        if level == 2:
            return unpack(landed(stream, 2, entry), B)
        held = HELD[level - 1]
        pieces = ws[stream][level - 1].buf.reshape(ROWS // held, held, N)
        total = (
            hit(entry, 0) * pieces[table[entry, 0]] + hit(entry, 1) * pieces[table[entry, 1]]
        )
        return jnp.where(core == 0, total, turned(total))

    def multiply(matrix, row, held, chunks):
        tall = min(held, B)
        totals = []
        for first in range(row, row + held, tall):
            total = None
            column = 0
            for right in chunks:
                depth = right.shape[0]
                left = matrix[2 * first : 2 * (first + tall), column : column + depth]
                part = dot(left, right)
                total = part if total is None else total + part
                column += depth
            totals.append(fold_narrow(total))
        return totals[0] if len(totals) == 1 else jnp.concatenate(totals, axis=0)

    def together(pair, before, after):
        before()

        def start(c):
            for gather in pair:
                gather.middle(c)

        both(start)
        for stream, gather in enumerate(pair):

            def rest(c, gather=gather):
                gather.close(c)
                gather.finish(c)

            both(rest)
            after(stream)

    send_update(0, 0, -acc_v[...])
    send_update(1, 0, turned(-acc_v[...]))

    def before_first():
        both(lambda c: [gather.middle(c) for gather in hs])
        store(y_v, solved_out)
        fill(1)
        loads[13].wait()
        widen(m_v, ms_v, 1, 0, HELD[0])
        loads[14].wait()
        widen(e_v, es_v, 1, 0, HELD[0])

    def nothing():
        pass

    piv_row = 0
    for level in range(1, LEVELS + 1):
        held = HELD[level - 1]
        rows = pl.ds(piv_row, held)
        last = level == LEVELS

        def pivots(stream, level=level, row=piv_row, held=held, last=last):
            place(stream, level)
            value = multiply(ms_v, row, held, [narrow(p_v[stream])])
            if not last:
                gather = zs[stream][level - 1]
                own = mine(gather)
                gather.buf[own] = pack(value)
                both(gather.begin)
            if stream == 0:
                z_v[row : row + held, :] = value
            else:
                z_v[row : row + held, :] = merged(z_v[row : row + held, :], value)

        together([ws[0][level - 1], ws[1][level - 1]], before_first if level == 1 else nothing, pivots)
        store(z_v.at[rows], front_out.at[rows])
        if last:
            break

        def prepare_next(level=level, row=piv_row, held=held):
            fill(level + 1)
            widen(m_v, ms_v, level + 1, row + held, HELD[level])
            if level + 1 < LEVELS:
                widen(e_v, es_v, level + 1, row + held, HELD[level])

        def updates(stream, level=level, row=piv_row, held=held):
            gather = zs[stream][level - 1]
            chunks = [
                narrow(unpack(gather.buf[y, z].reshape(4 * held, N), min(held, B)))
                for y in range(YS[level - 1])
                for z in range(ZS[level - 1])
            ]
            value = update_rows(stream, level) - multiply(es_v, row, held, chunks)
            send_update(stream, level, value)

        together([zs[0][level - 1], zs[1][level - 1]], prepare_next, updates)
        piv_row += held

    both(lambda c: [gather.drain(c) for gather in gathers])
    for copy in stores:
        copy.wait()


def tables(sub_pattern, sub_map, front_map):
    leaf = lax.axis_index("leaf")
    front = lax.axis_index("front")
    pivots = jnp.arange(PB, dtype=jnp.int32)
    places, flags = [], []
    maps = lax.dynamic_slice_in_dim(sub_map, leaf * 8, 8)
    wanted = jnp.concatenate([pivots, PB + 2 * front + jnp.arange(2, dtype=jnp.int32)])
    match = maps[None] == wanted[:, None, None]
    places.append(2 * jnp.arange(8, dtype=jnp.int32) + match[:, :, 1].astype(jnp.int32))
    flags.append(match.any(axis=2))
    for level in range(2, LEVELS + 1):
        held = HELD[level - 1]
        maps = lax.dynamic_slice_in_dim(
            front_map, MAP_AT[level - 2] + 2 * (leaf // 2 ** (level - 1)), 2
        )
        row = ((leaf % 2 ** (level - 1)) * 8 + front) * held
        wanted = jnp.concatenate([pivots, (PB + row // B)[None]])
        match = maps[None] == wanted[:, None, None]
        place = jnp.sum(match * jnp.arange(PB, dtype=jnp.int32), axis=2, dtype=jnp.int32)
        place = place + jnp.array([0, PB], jnp.int32)
        last = jnp.arange(PB + 1)[:, None] == PB
        unit = min(B, 2 * held)
        place = jnp.where(last, place * (B // unit) + row % B // unit, place)
        places.append(jnp.pad(place, ((0, 0), (0, 6))))
        flags.append(jnp.pad(match.any(axis=2), ((0, 0), (0, 6))))
    found = jnp.concatenate([jnp.concatenate(places), jnp.concatenate(flags).astype(jnp.int32)], axis=1)
    return jnp.concatenate([found, jnp.pad(sub_pattern[:, 1:], ((0, 0), (0, 15)))])


def per_device(
    sub_rhs, sub_dinv, sub_off, sub_pattern, sub_update, sub_map,
    front_rhs, piv_inverse, upd_factor, front_map,
):
    def wide(level, held):
        return pltpu.VMEM((YS[level - 1], ZS[level - 1], 4, 2, held, N), F32)

    scratch = [
        pltpu.VMEM((SB, B, N), F32),
        pltpu.VMEM((SB, B, B), F32),
        pltpu.VMEM((SB - 1, K, B, B), F32),
        pltpu.VMEM((2 * B, SB * B), F32),
        pltpu.VMEM((PROWS, ROWS), F32),
        pltpu.VMEM((UROWS, ROWS), F32),
        pltpu.VMEM((SB, B, N), F32),
        pltpu.VMEM((SB, B, 2 * N), BF16),
        pltpu.VMEM((2, 2 * B, 2 * B), BF16),
        pltpu.VMEM((2, B, N), F32),
        pltpu.VMEM((2 * B, N), F32),
        pltpu.VMEM((2, ROWS, N), F32),
        pltpu.VMEM((2 * PROWS, ROWS), BF16),
        pltpu.VMEM((2 * UROWS, ROWS), BF16),
        pltpu.VMEM((PROWS, N), F32),
    ]
    scratch += [wide(level, HELD[level - 1]) for level in range(1, 6)]
    for _ in range(2):
        scratch += [wide(1, B)]
        scratch += [wide(level + 1, HELD[level - 1] // 2) for level in range(1, 5)]
        scratch += [wide(level, HELD[level - 1] // 2) for level in range(1, 5)]
    copies = sum(COPIES) + 2 * (sum(COPIES) + sum(COPIES[:4]))
    scratch += [
        pltpu.SemaphoreType.DMA((15,)),
        pltpu.SemaphoreType.DMA((6,)),
        pltpu.SemaphoreType.DMA((copies,)),
        pltpu.SemaphoreType.DMA((copies,)),
    ]
    smem = pl.BlockSpec(memory_space=pltpu.SMEM)
    hbm = pl.BlockSpec(memory_space=pl.ANY)
    solved, fronts = pl.pallas_call(
        kernel,
        out_shape=(
            jax.ShapeDtypeStruct((SB, B, N), F32),
            jax.ShapeDtypeStruct((PROWS, N), F32),
        ),
        in_specs=[smem] + [hbm] * 7,
        out_specs=(hbm, hbm),
        scratch_shapes=scratch,
        compiler_params=pltpu.CompilerParams(
            collective_id=0, has_side_effects=True, vmem_limit_bytes=62 * 2**20
        ),
    )(
        tables(sub_pattern, sub_map, front_map),
        sub_rhs.reshape(SB, B, N), sub_dinv, sub_off, sub_update, front_rhs, piv_inverse, upd_factor,
    )
    return solved.reshape(SB * B, N), fronts


def solution(mesh):
    rows = P(("leaf", "front"), None)
    return jax.shard_map(
        per_device,
        mesh=mesh,
        in_specs=(
            rows,
            P(("leaf", "front"), None, None),
            P(("leaf", "front"), None, None, None),
            rows,
            rows,
            P(),
            rows,
            rows,
            rows,
            P(),
        ),
        out_specs=(rows, rows),
        check_vma=False,
    )
```

```python
import itertools

import jax
import jax.numpy as jnp
from jax import lax
from jax.experimental import pallas as pl
from jax.experimental.pallas import tpu as pltpu
from jax.sharding import PartitionSpec as P

B = 128
N = 128
SB = 24
K = 2
ROWS = 2048
PB = 16
LEVELS = 5
PROWS = 496
UROWS = 480
MAPROWS = 30
YS = (1, 1, 1, 2, 4)
ZS = (1, 2, 4, 4, 4)
HELD = (256, 128, 64, 32, 16)
MAP_AT = (0, 16, 24, 28)
ENTRY_AT = (None, 0, 18, 35, 52, 69)
MIXED = (("x", "zy"), ("zy", "x"))
SAME = (("x", "zy"), ("x", "zy"))
SENDS = (3, 7, 15, 10, 18)
COPIES = (7, 12, 22, 21, 37)
HALF = 64
COLUMNS_AT = 86
EARLY = 8
F32 = jnp.float32
BF16 = jnp.bfloat16


def split(value):
    high = value.astype(BF16)
    return high, (value - high.astype(F32)).astype(BF16)


def side(value):
    return jnp.concatenate(split(value), axis=1)


def stack(value):
    return jnp.concatenate(split(value), axis=0)


def dot(left, right):
    return jnp.dot(left, right, preferred_element_type=F32)


def fold(product):
    half = product.shape[0] // 2
    return product[:half, :N] + (product[:half, N:] + product[half:, :N])


def low_half(shape):
    return lax.broadcasted_iota(jnp.int32, shape, len(shape) - 1) < HALF


def turned(value):
    return pltpu.roll(value, HALF, 1)


def choose(low, high):
    return jnp.where(low_half(low.shape), low, high)


def pairs(value, unit):
    many = value.shape[0]
    blocks = value.reshape(many // unit, unit, N)
    shape = (many // 2, N)
    return blocks[:, : unit // 2].reshape(shape), blocks[:, unit // 2 :].reshape(shape)


def streams_of(value, unit):
    lower, upper = pairs(value, unit)
    return choose(lower, turned(upper)), choose(turned(lower), upper)


def pack(value, unit):
    return choose(*pairs(value, unit))


def operand(packed, unit):
    high = packed.astype(BF16).astype(F32)
    low = turned(packed - high)
    shape = (2 * packed.shape[0] // unit, unit // 2, N)
    pair = [choose(high, low).reshape(shape), choose(low, high).reshape(shape)]
    return jnp.concatenate(pair, axis=1).reshape(2 * packed.shape[0], N).astype(BF16)


def fold_both(product):
    half = product.shape[0] // 2
    total = product[:half] + product[half:]
    return total + turned(total)


class Gather:
    def __init__(self, buf, send, recv, base, level, at, order):
        self.buf, self.send, self.recv, self.at = buf, send, recv, at
        self.base, self.level, eager = base, level, level < 4
        self.size = {"x": 4, "z": ZS[level - 1], "y": YS[level - 1]}
        self.order, self.eager = order, eager
        self.own = {d: 0 if self.size[d] == 1 else at[d] % self.size[d] for d in "yzx"}

    def sets(self, core):
        found = ["".join(d for d in dims if self.size[d] > 1) for dims in self.order[core]]
        return found[0] or found[1], found[1] if found[0] else ""

    def hops(self, dims):
        steps = [
            dict(zip(dims, offsets))
            for offsets in itertools.product(*(range(self.size[d]) for d in dims))
            if any(offsets)
        ]
        return sorted(steps, key=lambda step: sum(min(o, self.size[d] - o) for d, o in step.items()))

    def moved(self, dim, offset):
        here = self.at[dim]
        if offset == 0:
            return here
        if self.size[dim] == 4:
            return (here + offset) % 4
        return here + 1 - 2 * (here % 2)

    def origin(self, step):
        return {
            d: self.moved(d, -o % self.size[d]) % self.size[d] for d, o in step.items()
        }

    def view(self, core, full="", **places):
        place = {**self.own, **places}
        index = [slice(None) if d in full else place[d] for d in "yzx"]
        return self.buf.at[index[0], index[1], index[2], core]

    def copy(self, view, which, **changes):
        place = {**self.at, **changes}
        return pltpu.make_async_remote_copy(
            src_ref=view,
            dst_ref=view,
            send_sem=self.send.at[self.base + which],
            recv_sem=self.recv.at[self.base + which],
            device_id=(place["y"] * 4 + place["z"], place["x"] * 2 + place["core"]),
            device_id_type=pl.DeviceIdType.MESH,
        )

    def to(self, step):
        return {d: self.moved(d, o) for d, o in step.items()}

    def out(self, view, which, core, step):
        return lambda: self.copy(view, which, core=core, **self.to(step))

    def across(self, view, which, core):
        return lambda: self.copy(view, which, core=1 - core)

    def plan(self, core):
        first, second = self.sets(core)
        near, far = self.hops(first), self.hops(second) if second else []
        cross = SENDS[self.level - 1]
        begin = [self.out(self.view(core), i, core, step) for i, step in enumerate(near)]
        used = len(near)
        mine = [(self.view(core), cross)]
        middle, close = [], []
        held = [{}] + [self.origin(step) for step in near]
        sets = [held[i : i + 1] for i in range(len(held))] if self.eager else [held]
        sends = []
        for group in sets:
            view = self.view(core, **group[0]) if self.eager else self.view(core, first)
            sends.append([self.out(view, used + j, core, step) for j, step in enumerate(far)])
            used += len(far)
        if self.eager:
            begin += sends[0]
        for i, step in enumerate(near):
            view = self.view(core, **held[i + 1])
            mine.append((view, cross + 1 + i))
            after = sends[i + 1] if self.eager else sends[0] if i == len(near) - 1 else []
            middle.append(([(view, i)], after + [self.across(view, cross + 1 + i, core)]))
        if not second:
            middle = [(wait, [start[-1]]) for wait, start in middle]
        for j, step in enumerate(far):
            origin = self.origin(step)
            waits = []
            for g, group in enumerate(sets):
                if self.eager:
                    view = self.view(core, **{**group[0], **origin})
                else:
                    view = self.view(core, first, **origin)
                waits.append((view, len(near) + g * len(far) + j))
            view, which = self.view(core, first, **origin), cross + 1 + len(near) + j
            mine.append((view, which))
            close.append((waits, [self.across(view, which, core)]))
        begin.append(self.across(self.view(core), cross, core))
        return begin, middle, close, mine

    def begin(self, core):
        for make in self.plan(core)[0]:
            make().start()

    def follow(self, steps, core):
        for waits, starts in steps:
            for view, which in waits:
                self.copy(view, which, core=1 - core).wait_recv()
            for make in starts:
                make().start()

    def middle(self, core):
        self.follow(self.plan(core)[1], core)

    def close(self, core):
        self.follow(self.plan(core)[2], core)

    def finish(self, core):
        for view, which in self.plan(1 - core)[3]:
            self.copy(view, which, core=1 - core).wait_recv()

    def drain(self, core):
        begin, middle, close, _ = self.plan(core)
        for make in begin + [make for _, starts in middle + close for make in starts]:
            make().wait_send()


def kernel(
    table,
    rhs, dinv, off, update, front_rhs, piv, factor,
    solved_out, front_out,
    b_v, d_v, l_v, u_v, m_v, e_v, y_v, yhl_v, g_v, c_v, acc_v, p_v, rhs_v, ms_v, es_v, z_v,
    h1, h2, h3, h4, h5, *rest,
):
    leaf = lax.axis_index("leaf")
    front = lax.axis_index("front")
    core = front % 2
    at = {"y": leaf // 4, "z": leaf % 4, "x": front // 2, "core": core}

    def both(step):
        for which in (0, 1):
            @pl.when(core == which)
            def _():
                step(which)

    streams, (load_sem, store_sem, send, recv) = rest[:18], rest[18:]
    levels = [1, 2, 3, 4, 5] + 2 * [1, 2, 3, 4, 5, 1, 2, 3, 4]
    gathers = []
    base = 0
    for buf, level in zip((h1, h2, h3, h4, h5, *streams), levels):
        order = SAME if len(gathers) < 5 else MIXED
        gathers.append(Gather(buf, send, recv, base, level, at, order))
        base += COPIES[level - 1]
    hs = gathers[:5]
    ws = (gathers[5:10], gathers[14:19])
    zs = (gathers[10:14], gathers[19:23])

    def mine(gather):
        own = gather.own
        return (own["y"], own["z"], own["x"], core)

    loads = []

    def load(source, target):
        copy = pltpu.make_async_copy(source, target, load_sem.at[len(loads)])
        copy.start()
        loads.append(copy)

    row = 0
    for gather, held in zip(hs, HELD):
        load(front_rhs.at[pl.ds(row, held)], gather.buf.at[mine(gather)])
        row += held
    for first, many in ((0, EARLY), (EARLY, SB - EARLY)):
        load(dinv.at[pl.ds(first, many)], d_v.at[pl.ds(first, many)])
        load(off.at[pl.ds(first, many - first // EARLY)], l_v.at[pl.ds(first, many - first // EARLY)])
        load(rhs.at[pl.ds(first, many)], b_v.at[pl.ds(first, many)])
        columns = pl.ds(first * B, many * B)
        load(update.at[:, columns], u_v.at[:, columns])
    load(piv, m_v)
    load(factor, e_v)

    barrier = pltpu.get_barrier_semaphore()
    peers = [(at["y"], at["z"], (at["x"] + o) % 4, core) for o in (1, 2, 3)]
    peers += [
        ((at["y"] + oy) % 4, (at["z"] + oz) % 4, at["x"], core)
        for oy in range(4)
        for oz in range(4)
        if oy or oz
    ]
    peers.append((at["y"], at["z"], at["x"], 1 - core))
    for y, z, x, c in peers:
        pl.semaphore_signal(
            barrier, inc=1, device_id=(y * 4 + z, x * 2 + c), device_id_type=pl.DeviceIdType.MESH
        )
    pl.semaphore_wait(barrier, len(peers))

    for copy in loads[:5]:
        copy.wait()
    both(lambda c: [gather.begin(c) for gather in hs])
    for copy in loads[5:9]:
        copy.wait()

    def prepare(block, slot):
        high, low = split(d_v[block])
        wide = jnp.concatenate([l_v[block - 1, 0], l_v[block - 1, 1], b_v[block]], axis=1)
        wide_high, wide_low = split(wide)
        first = dot(jnp.concatenate([high, low], axis=0), wide_high)
        product = first[:B] + (first[B:] + dot(high, wide_low))
        g_v[slot] = stack(product[:, : 2 * B])
        c_v[slot] = product[:, 2 * B :]

    def keep(block, value):
        y_v[block] = value
        yhl_v[block] = side(value)

    def couple(block):
        columns = pl.ds(pl.multiple_of(block * B, B), B)
        acc_v[...] += fold(dot(stack(u_v[:, columns]), yhl_v[block]))

    keep(0, fold(dot(stack(d_v[0]), side(b_v[0]))))
    prepare(1, 1)
    acc_v[...] = jnp.zeros_like(acc_v)

    def advance(block, carry):
        slot = lax.rem(block, 2)
        known = jnp.concatenate([yhl_v[block - 1], yhl_v[table[COLUMNS_AT + block - 1, 0]]], axis=0)
        value = c_v[slot] - fold(dot(g_v[slot], known))
        couple(block - 1)
        prepare(jnp.minimum(block + 1, SB - 1), 1 - slot)
        keep(block, value)
        return carry

    lax.fori_loop(1, EARLY - 1, advance, 0)
    for copy in loads[9:13]:
        copy.wait()
    lax.fori_loop(EARLY - 1, SB, advance, 0)
    couple(SB - 1)

    stores = []

    def store(source, target):
        copy = pltpu.make_async_copy(source, target, store_sem.at[len(stores)])
        copy.start()
        stores.append(copy)

    def widen(source, target, row, held):
        tall = min(held, B)
        for first in range(row, row + held, tall):
            target[2 * first : 2 * (first + tall), :] = stack(source[first : first + tall, :])

    def unit_of(level):
        return B if level == 1 else min(B, HELD[level - 2])

    def fill(level):
        gather = hs[level - 1]

        def rest(c):
            gather.close(c)
            gather.finish(c)

        both(rest)
        held = HELD[level - 1]
        many = 8 * held
        for y in range(YS[level - 1]):
            for z in range(ZS[level - 1]):
                first = (y * ZS[level - 1] + z) * many
                rows = slice(first // 2, (first + many) // 2)
                parts = streams_of(gather.buf[y, z].reshape(many, N), unit_of(level))
                p_v[0, rows, :], p_v[1, rows, :] = parts

    def send_update(stream, level, value):
        gather = ws[stream][level]
        own = mine(gather)
        gather.buf[own] = value
        both(gather.begin)

    def hit(entry, which):
        return table[entry, 8 + which].astype(F32)

    def landed(stream, level, entry):
        gather = ws[stream][level - 1]
        blocks = gather.buf.reshape(PB if level == 1 else 2 * PB, HALF, N)
        total = hit(entry, 0) * blocks[table[entry, 0]]
        for child in range(1, 8 if level == 1 else 2):
            total = total + hit(entry, child) * blocks[table[entry, child]]
        return total

    def place(stream, level):
        def body(block, carry):
            packed = pl.ds(pl.multiple_of(block * HALF, HALF), HALF)
            rows = pl.ds(pl.multiple_of(block * B, B), B)
            total = p_v[stream, packed, :] + landed(stream, level, ENTRY_AT[level] + block)
            rhs_v[rows, :] = operand(total, unit_of(level))
            return carry

        lax.fori_loop(0, PB, body, 0, unroll=4)

    def update_rows(stream, level):
        entry = ENTRY_AT[level] + PB
        if level == 1:
            return jnp.concatenate([landed(stream, 1, entry + i) for i in (0, 1)], axis=0)
        if level == 2:
            return landed(stream, 2, entry)
        held = HELD[level - 1]
        pieces = ws[stream][level - 1].buf.reshape(ROWS // held, held, N)
        total = (
            hit(entry, 0) * pieces[table[entry, 0]] + hit(entry, 1) * pieces[table[entry, 1]]
        )
        lower, upper = pairs(jnp.where(core == 0, total, turned(total)), held)
        return choose(lower, turned(upper))

    def multiply(matrix, row, held, chunks):
        tall = min(held, B)
        totals = []
        for first in range(row, row + held, tall):
            total = None
            column = 0
            for right in chunks:
                depth = right.shape[0]
                left = matrix[2 * first : 2 * (first + tall), column : column + depth]
                part = dot(left, right)
                total = part if total is None else total + part
                column += depth
            totals.append(fold_both(total))
        return totals[0] if len(totals) == 1 else jnp.concatenate(totals, axis=0)

    def together(pair, before, after):
        before()

        def start(c):
            for gather in pair:
                gather.middle(c)

        both(start)
        for stream, gather in enumerate(pair):

            def rest(c, gather=gather):
                gather.close(c)
                gather.finish(c)

            both(rest)
            after(stream)

    for stream, value in enumerate(streams_of(-acc_v[...], B)):
        send_update(stream, 0, value)

    def before_first():
        both(lambda c: [gather.middle(c) for gather in hs])
        store(y_v, solved_out)
        fill(1)
        loads[13].wait()
        widen(m_v, ms_v, 0, HELD[0])
        loads[14].wait()
        widen(e_v, es_v, 0, HELD[0])

    def nothing():
        pass

    piv_row = 0
    for level in range(1, LEVELS + 1):
        held = HELD[level - 1]
        rows = pl.ds(piv_row, held)
        last = level == LEVELS

        def pivots(stream, level=level, row=piv_row, held=held, last=last):
            place(stream, level)
            value = multiply(ms_v, row, held, [rhs_v[...]])
            if not last:
                gather = zs[stream][level - 1]
                own = mine(gather)
                gather.buf[own] = pack(value, min(held, B))
                both(gather.begin)
            if stream == 0:
                z_v[row : row + held, :] = value
            else:
                z_v[row : row + held, :] = choose(z_v[row : row + held, :], value)

        together([ws[0][level - 1], ws[1][level - 1]], before_first if level == 1 else nothing, pivots)
        store(z_v.at[rows], front_out.at[rows])
        if last:
            break

        def prepare_next(level=level, row=piv_row, held=held):
            fill(level + 1)
            widen(m_v, ms_v, row + held, HELD[level])
            if level + 1 < LEVELS:
                widen(e_v, es_v, row + held, HELD[level])

        def updates(stream, level=level, row=piv_row, held=held):
            gather = zs[stream][level - 1]
            chunks = [
                operand(gather.buf[y, z].reshape(4 * held, N), min(held, B))
                for y in range(YS[level - 1])
                for z in range(ZS[level - 1])
            ]
            value = pack(multiply(es_v, row, held, chunks), min(held, B))
            send_update(stream, level, update_rows(stream, level) - value)

        together([zs[0][level - 1], zs[1][level - 1]], prepare_next, updates)
        piv_row += held

    both(lambda c: [gather.drain(c) for gather in gathers])
    for copy in stores:
        copy.wait()


def tables(sub_pattern, sub_map, front_map):
    leaf = lax.axis_index("leaf")
    front = lax.axis_index("front")
    pivots = jnp.arange(PB, dtype=jnp.int32)
    places, flags = [], []
    maps = lax.dynamic_slice_in_dim(sub_map, leaf * 8, 8)
    wanted = jnp.concatenate([pivots, PB + 2 * front + jnp.arange(2, dtype=jnp.int32)])
    match = maps[None] == wanted[:, None, None]
    places.append(2 * jnp.arange(8, dtype=jnp.int32) + match[:, :, 1].astype(jnp.int32))
    flags.append(match.any(axis=2))
    for level in range(2, LEVELS + 1):
        held = HELD[level - 1]
        maps = lax.dynamic_slice_in_dim(
            front_map, MAP_AT[level - 2] + 2 * (leaf // 2 ** (level - 1)), 2
        )
        row = ((leaf % 2 ** (level - 1)) * 8 + front) * held
        wanted = jnp.concatenate([pivots, (PB + row // B)[None]])
        match = maps[None] == wanted[:, None, None]
        place = jnp.sum(match * jnp.arange(PB, dtype=jnp.int32), axis=2, dtype=jnp.int32)
        place = place + jnp.array([0, PB], jnp.int32)
        last = jnp.arange(PB + 1)[:, None] == PB
        unit = min(B, 2 * held)
        place = jnp.where(last, place * (B // unit) + row % B // unit, place)
        places.append(jnp.pad(place, ((0, 0), (0, 6))))
        flags.append(jnp.pad(match.any(axis=2), ((0, 0), (0, 6))))
    found = jnp.concatenate([jnp.concatenate(places), jnp.concatenate(flags).astype(jnp.int32)], axis=1)
    return jnp.concatenate([found, jnp.pad(sub_pattern[:, 1:], ((0, 0), (0, 15)))])


def per_device(
    sub_rhs, sub_dinv, sub_off, sub_pattern, sub_update, sub_map,
    front_rhs, piv_inverse, upd_factor, front_map,
):
    def wide(level, held):
        return pltpu.VMEM((YS[level - 1], ZS[level - 1], 4, 2, held, N), F32)

    scratch = [
        pltpu.VMEM((SB, B, N), F32),
        pltpu.VMEM((SB, B, B), F32),
        pltpu.VMEM((SB - 1, K, B, B), F32),
        pltpu.VMEM((2 * B, SB * B), F32),
        pltpu.VMEM((PROWS, ROWS), F32),
        pltpu.VMEM((UROWS, ROWS), F32),
        pltpu.VMEM((SB, B, N), F32),
        pltpu.VMEM((SB, B, 2 * N), BF16),
        pltpu.VMEM((2, 2 * B, 2 * B), BF16),
        pltpu.VMEM((2, B, N), F32),
        pltpu.VMEM((2 * B, N), F32),
        pltpu.VMEM((2, ROWS // 2, N), F32),
        pltpu.VMEM((ROWS, N), BF16),
        pltpu.VMEM((2 * PROWS, ROWS), BF16),
        pltpu.VMEM((2 * UROWS, ROWS), BF16),
        pltpu.VMEM((PROWS, N), F32),
    ]
    scratch += [wide(level, HELD[level - 1]) for level in range(1, 6)]
    for _ in range(2):
        scratch += [wide(1, B)]
        scratch += [wide(level + 1, HELD[level - 1] // 2) for level in range(1, 5)]
        scratch += [wide(level, HELD[level - 1] // 2) for level in range(1, 5)]
    copies = sum(COPIES) + 2 * (sum(COPIES) + sum(COPIES[:4]))
    scratch += [
        pltpu.SemaphoreType.DMA((15,)),
        pltpu.SemaphoreType.DMA((6,)),
        pltpu.SemaphoreType.DMA((copies,)),
        pltpu.SemaphoreType.DMA((copies,)),
    ]
    smem = pl.BlockSpec(memory_space=pltpu.SMEM)
    hbm = pl.BlockSpec(memory_space=pl.ANY)
    solved, fronts = pl.pallas_call(
        kernel,
        out_shape=(
            jax.ShapeDtypeStruct((SB, B, N), F32),
            jax.ShapeDtypeStruct((PROWS, N), F32),
        ),
        in_specs=[smem] + [hbm] * 7,
        out_specs=(hbm, hbm),
        scratch_shapes=scratch,
        compiler_params=pltpu.CompilerParams(
            collective_id=0, has_side_effects=True, vmem_limit_bytes=62 * 2**20
        ),
    )(
        tables(sub_pattern, sub_map, front_map),
        sub_rhs.reshape(SB, B, N), sub_dinv, sub_off, sub_update, front_rhs, piv_inverse, upd_factor,
    )
    return solved.reshape(SB * B, N), fronts


def solution(mesh):
    rows = P(("leaf", "front"), None)
    return jax.shard_map(
        per_device,
        mesh=mesh,
        in_specs=(
            rows,
            P(("leaf", "front"), None, None),
            P(("leaf", "front"), None, None, None),
            rows,
            rows,
            P(),
            rows,
            rows,
            rows,
            P(),
        ),
        out_specs=(rows, rows),
        check_vma=False,
    )
```

```python
import itertools

import jax
import jax.numpy as jnp
from jax import lax
from jax.experimental import pallas as pl
from jax.experimental.pallas import tpu as pltpu
from jax.sharding import PartitionSpec as P

B = 128
N = 128
SB = 24
K = 2
ROWS = 2048
PB = 16
LEVELS = 5
PROWS = 496
UROWS = 480
MAPROWS = 30
YS = (1, 1, 1, 2, 4)
ZS = (1, 2, 4, 4, 4)
HELD = (256, 128, 64, 32, 16)
MAP_AT = (0, 16, 24, 28)
ENTRY_AT = (None, 0, 18, 35, 52, 69)
MIXED = (("x", "zy"), ("zy", "x"))
SAME = (("x", "zy"), ("x", "zy"))
SENDS = (3, 7, 15, 10, 18)
HALF = 64
COLUMNS_AT = 86
EARLY = 8
F32 = jnp.float32
BF16 = jnp.bfloat16


def split(value):
    high = value.astype(BF16)
    return high, (value - high.astype(F32)).astype(BF16)


def side(value):
    return jnp.concatenate(split(value), axis=1)


def stack(value):
    return jnp.concatenate(split(value), axis=0)


def dot(left, right):
    return jnp.dot(left, right, preferred_element_type=F32)


def fold(product):
    half = product.shape[0] // 2
    return product[:half, :N] + (product[:half, N:] + product[half:, :N])


def low_half(shape):
    return lax.broadcasted_iota(jnp.int32, shape, len(shape) - 1) < HALF


def turned(value):
    return pltpu.roll(value, HALF, 1)


def choose(low, high):
    return jnp.where(low_half(low.shape), low, high)


def pairs(value, unit):
    many = value.shape[0]
    blocks = value.reshape(many // unit, unit, N)
    shape = (many // 2, N)
    return blocks[:, : unit // 2].reshape(shape), blocks[:, unit // 2 :].reshape(shape)


def streams_of(value, unit):
    lower, upper = pairs(value, unit)
    return choose(lower, turned(upper)), choose(turned(lower), upper)


def pack(value, unit):
    return choose(*pairs(value, unit))


def operand(packed, unit):
    high = packed.astype(BF16).astype(F32)
    low = turned(packed - high)
    shape = (2 * packed.shape[0] // unit, unit // 2, N)
    pair = [choose(high, low).reshape(shape), choose(low, high).reshape(shape)]
    return jnp.concatenate(pair, axis=1).reshape(2 * packed.shape[0], N).astype(BF16)


def fold_both(product):
    half = product.shape[0] // 2
    total = product[:half] + product[half:]
    return total + turned(total)


class Gather:
    def __init__(self, buf, send, recv, level, at, order):
        self.buf, self.send, self.recv, self.at = buf, send, recv, at
        self.level, eager = level, level < 4
        self.size = {"x": 4, "z": ZS[level - 1], "y": YS[level - 1]}
        self.order, self.eager = order, eager
        self.own = {d: 0 if self.size[d] == 1 else at[d] % self.size[d] for d in "yzx"}

    def sets(self, core):
        found = ["".join(d for d in dims if self.size[d] > 1) for dims in self.order[core]]
        return found[0] or found[1], found[1] if found[0] else ""

    def hops(self, dims):
        steps = [
            dict(zip(dims, offsets))
            for offsets in itertools.product(*(range(self.size[d]) for d in dims))
            if any(offsets)
        ]
        return sorted(steps, key=lambda step: sum(min(o, self.size[d] - o) for d, o in step.items()))

    def moved(self, dim, offset):
        here = self.at[dim]
        if offset == 0:
            return here
        if self.size[dim] == 4:
            return (here + offset) % 4
        return here + 1 - 2 * (here % 2)

    def origin(self, step):
        return {
            d: self.moved(d, -o % self.size[d]) % self.size[d] for d, o in step.items()
        }

    def view(self, core, full="", **places):
        place = {**self.own, **places}
        index = [slice(None) if d in full else place[d] for d in "yzx"]
        return self.buf.at[index[0], index[1], index[2], core]

    def copy(self, view, which, **changes):
        place = {**self.at, **changes}
        return pltpu.make_async_remote_copy(
            src_ref=view,
            dst_ref=view,
            send_sem=self.send,
            recv_sem=self.recv.at[which],
            device_id=(place["y"] * 4 + place["z"], place["x"] * 2 + place["core"]),
            device_id_type=pl.DeviceIdType.MESH,
        )

    def to(self, step):
        return {d: self.moved(d, o) for d, o in step.items()}

    def out(self, view, which, core, step):
        return lambda: self.copy(view, which, core=core, **self.to(step))

    def across(self, view, which, core):
        return lambda: self.copy(view, which, core=1 - core)

    def plan(self, core):
        first, second = self.sets(core)
        near, far = self.hops(first), self.hops(second) if second else []
        cross = SENDS[self.level - 1]
        begin = [self.out(self.view(core), i, core, step) for i, step in enumerate(near)]
        used = len(near)
        middle, close = [], []
        held = [{}] + [self.origin(step) for step in near]
        sets = [held[i : i + 1] for i in range(len(held))] if self.eager else [held]
        sends = []
        for group in sets:
            view = self.view(core, **group[0]) if self.eager else self.view(core, first)
            sends.append([self.out(view, used + j, core, step) for j, step in enumerate(far)])
            used += len(far)
        if self.eager:
            begin += sends[0]
        for i, step in enumerate(near):
            view = self.view(core, **held[i + 1])
            after = sends[i + 1] if self.eager else sends[0] if i == len(near) - 1 else []
            middle.append(([(view, i)], after + [self.across(view, cross, core)]))
        if not second:
            middle = [(wait, [start[-1]]) for wait, start in middle]
        for j, step in enumerate(far):
            origin = self.origin(step)
            waits = []
            for g, group in enumerate(sets):
                if self.eager:
                    view = self.view(core, **{**group[0], **origin})
                else:
                    view = self.view(core, first, **origin)
                waits.append((view, len(near) + g * len(far) + j))
            view = self.view(core, first, **origin)
            close.append((waits, [self.across(view, cross, core)]))
        begin.append(self.across(self.view(core), cross, core))
        return begin, middle, close

    def begin(self, core):
        for make in self.plan(core)[0]:
            make().start()

    def follow(self, steps, core):
        for waits, starts in steps:
            for view, which in waits:
                self.copy(view, which, core=1 - core).wait_recv()
            for make in starts:
                make().start()

    def middle(self, core):
        self.follow(self.plan(core)[1], core)

    def close(self, core):
        self.follow(self.plan(core)[2], core)

    def finish(self, core):
        half = self.view(1 - core, "yzx")
        self.copy(half, SENDS[self.level - 1], core=1 - core).wait_recv()

    def drain(self, spare):
        rows = (8 * self.size["y"] * self.size["z"] - 1) * self.buf.shape[-2]
        view = spare.at[pl.ds(0, rows)]
        self.copy(view, 0, core=1 - self.at["core"]).wait_send()


def kernel(
    table,
    rhs, dinv, off, update, front_rhs, piv, factor,
    solved_out, front_out,
    b_v, d_v, l_v, u_v, m_v, e_v, y_v, yhl_v, g_v, c_v, acc_v, p_v, rhs_v, ms_v, es_v, z_v,
    h1, h2, h3, h4, h5, *rest,
):
    leaf = lax.axis_index("leaf")
    front = lax.axis_index("front")
    core = front % 2
    at = {"y": leaf // 4, "z": leaf % 4, "x": front // 2, "core": core}

    def both(step):
        for which in (0, 1):
            @pl.when(core == which)
            def _():
                step(which)

    streams, (load_sem, store_sem, send, recv) = rest[:18], rest[18:]
    levels = [1, 2, 3, 4, 5] + 2 * [1, 2, 3, 4, 5, 1, 2, 3, 4]
    gathers = []
    base = 0
    for buf, level in zip((h1, h2, h3, h4, h5, *streams), levels):
        order = SAME if len(gathers) < 5 else MIXED
        copies = SENDS[level - 1] + 1
        gathers.append(
            Gather(buf, send.at[len(gathers)], recv.at[pl.ds(base, copies)], level, at, order)
        )
        base += copies
    hs = gathers[:5]
    ws = (gathers[5:10], gathers[14:19])
    zs = (gathers[10:14], gathers[19:23])

    def mine(gather):
        own = gather.own
        return (own["y"], own["z"], own["x"], core)

    loads = []

    def load(source, target):
        copy = pltpu.make_async_copy(source, target, load_sem.at[len(loads)])
        copy.start()
        loads.append(copy)

    row = 0
    for gather, held in zip(hs, HELD):
        load(front_rhs.at[pl.ds(row, held)], gather.buf.at[mine(gather)])
        row += held
    for first, many in ((0, EARLY), (EARLY, SB - EARLY)):
        load(dinv.at[pl.ds(first, many)], d_v.at[pl.ds(first, many)])
        load(off.at[pl.ds(first, many - first // EARLY)], l_v.at[pl.ds(first, many - first // EARLY)])
        load(rhs.at[pl.ds(first, many)], b_v.at[pl.ds(first, many)])
        columns = pl.ds(first * B, many * B)
        load(update.at[:, columns], u_v.at[:, columns])
    load(piv, m_v)
    load(factor, e_v)

    barrier = pltpu.get_barrier_semaphore()
    peers = [(at["y"], at["z"], (at["x"] + o) % 4, core) for o in (1, 2, 3)]
    peers += [
        ((at["y"] + oy) % 4, (at["z"] + oz) % 4, at["x"], core)
        for oy in range(4)
        for oz in range(4)
        if oy or oz
    ]
    peers.append((at["y"], at["z"], at["x"], 1 - core))
    for y, z, x, c in peers:
        pl.semaphore_signal(
            barrier, inc=1, device_id=(y * 4 + z, x * 2 + c), device_id_type=pl.DeviceIdType.MESH
        )
    pl.semaphore_wait(barrier, len(peers))

    for copy in loads[:5]:
        copy.wait()
    both(lambda c: [gather.begin(c) for gather in hs])
    for copy in loads[5:9]:
        copy.wait()

    def prepare(block, slot):
        high, low = split(d_v[block])
        wide = jnp.concatenate([l_v[block - 1, 0], l_v[block - 1, 1], b_v[block]], axis=1)
        wide_high, wide_low = split(wide)
        first = dot(jnp.concatenate([high, low], axis=0), wide_high)
        product = first[:B] + (first[B:] + dot(high, wide_low))
        g_v[slot] = stack(product[:, : 2 * B])
        c_v[slot] = product[:, 2 * B :]

    def keep(block, value):
        y_v[block] = value
        yhl_v[block] = side(value)

    def couple(block):
        columns = pl.ds(pl.multiple_of(block * B, B), B)
        acc_v[...] += fold(dot(stack(u_v[:, columns]), yhl_v[block]))

    keep(0, fold(dot(stack(d_v[0]), side(b_v[0]))))
    prepare(1, 1)
    acc_v[...] = jnp.zeros_like(acc_v)

    def advance(block, carry):
        slot = lax.rem(block, 2)
        known = jnp.concatenate([yhl_v[block - 1], yhl_v[table[COLUMNS_AT + block - 1, 0]]], axis=0)
        value = c_v[slot] - fold(dot(g_v[slot], known))
        couple(block - 1)
        prepare(jnp.minimum(block + 1, SB - 1), 1 - slot)
        keep(block, value)
        return carry

    lax.fori_loop(1, EARLY - 1, advance, 0)
    for copy in loads[9:13]:
        copy.wait()
    lax.fori_loop(EARLY - 1, SB, advance, 0)
    couple(SB - 1)

    stores = []

    def store(source, target):
        copy = pltpu.make_async_copy(source, target, store_sem.at[len(stores)])
        copy.start()
        stores.append(copy)

    def widen(source, target, row, held):
        tall = min(held, B)
        for first in range(row, row + held, tall):
            target[2 * first : 2 * (first + tall), :] = stack(source[first : first + tall, :])

    def unit_of(level):
        return B if level == 1 else min(B, HELD[level - 2])

    def fill(level):
        gather = hs[level - 1]

        def rest(c):
            gather.close(c)
            gather.finish(c)

        both(rest)
        held = HELD[level - 1]
        many = 8 * held
        for y in range(YS[level - 1]):
            for z in range(ZS[level - 1]):
                first = (y * ZS[level - 1] + z) * many
                rows = slice(first // 2, (first + many) // 2)
                parts = streams_of(gather.buf[y, z].reshape(many, N), unit_of(level))
                p_v[0, rows, :], p_v[1, rows, :] = parts

    def send_update(stream, level, value):
        gather = ws[stream][level]
        own = mine(gather)
        gather.buf[own] = value
        both(gather.begin)

    def hit(entry, which):
        return table[entry, 8 + which].astype(F32)

    def landed(stream, level, entry):
        gather = ws[stream][level - 1]
        blocks = gather.buf.reshape(PB if level == 1 else 2 * PB, HALF, N)
        total = hit(entry, 0) * blocks[table[entry, 0]]
        for child in range(1, 8 if level == 1 else 2):
            total = total + hit(entry, child) * blocks[table[entry, child]]
        return total

    def place(stream, level):
        def body(block, carry):
            packed = pl.ds(pl.multiple_of(block * HALF, HALF), HALF)
            rows = pl.ds(pl.multiple_of(block * B, B), B)
            total = p_v[stream, packed, :] + landed(stream, level, ENTRY_AT[level] + block)
            rhs_v[rows, :] = operand(total, unit_of(level))
            return carry

        lax.fori_loop(0, PB, body, 0, unroll=4)

    def update_rows(stream, level):
        entry = ENTRY_AT[level] + PB
        if level == 1:
            return jnp.concatenate([landed(stream, 1, entry + i) for i in (0, 1)], axis=0)
        if level == 2:
            return landed(stream, 2, entry)
        held = HELD[level - 1]
        pieces = ws[stream][level - 1].buf.reshape(ROWS // held, held, N)
        total = (
            hit(entry, 0) * pieces[table[entry, 0]] + hit(entry, 1) * pieces[table[entry, 1]]
        )
        lower, upper = pairs(jnp.where(core == 0, total, turned(total)), held)
        return choose(lower, turned(upper))

    def multiply(matrix, row, held, chunks):
        tall = min(held, B)
        totals = []
        for first in range(row, row + held, tall):
            total = None
            column = 0
            for right in chunks:
                depth = right.shape[0]
                left = matrix[2 * first : 2 * (first + tall), column : column + depth]
                part = dot(left, right)
                total = part if total is None else total + part
                column += depth
            totals.append(fold_both(total))
        return totals[0] if len(totals) == 1 else jnp.concatenate(totals, axis=0)

    def together(pair, before, after):
        before()

        def start(c):
            for gather in pair:
                gather.middle(c)

        both(start)
        for stream, gather in enumerate(pair):

            def rest(c, gather=gather):
                gather.close(c)
                gather.finish(c)

            both(rest)
            after(stream)

    for stream, value in enumerate(streams_of(-acc_v[...], B)):
        send_update(stream, 0, value)

    def before_first():
        both(lambda c: [gather.middle(c) for gather in hs])
        store(y_v, solved_out)
        fill(1)
        loads[13].wait()
        widen(m_v, ms_v, 0, HELD[0])
        loads[14].wait()
        widen(e_v, es_v, 0, HELD[0])

    def nothing():
        pass

    piv_row = 0
    for level in range(1, LEVELS + 1):
        held = HELD[level - 1]
        rows = pl.ds(piv_row, held)
        last = level == LEVELS

        def pivots(stream, level=level, row=piv_row, held=held, last=last):
            place(stream, level)
            value = multiply(ms_v, row, held, [rhs_v[...]])
            if not last:
                gather = zs[stream][level - 1]
                own = mine(gather)
                gather.buf[own] = pack(value, min(held, B))
                both(gather.begin)
            if stream == 0:
                z_v[row : row + held, :] = value
            else:
                z_v[row : row + held, :] = choose(z_v[row : row + held, :], value)

        together([ws[0][level - 1], ws[1][level - 1]], before_first if level == 1 else nothing, pivots)
        store(z_v.at[rows], front_out.at[rows])
        if last:
            break

        def prepare_next(level=level, row=piv_row, held=held):
            fill(level + 1)
            widen(m_v, ms_v, row + held, HELD[level])
            if level + 1 < LEVELS:
                widen(e_v, es_v, row + held, HELD[level])

        def updates(stream, level=level, row=piv_row, held=held):
            gather = zs[stream][level - 1]
            chunks = [
                operand(gather.buf[y, z].reshape(4 * held, N), min(held, B))
                for y in range(YS[level - 1])
                for z in range(ZS[level - 1])
            ]
            value = pack(multiply(es_v, row, held, chunks), min(held, B))
            send_update(stream, level, update_rows(stream, level) - value)

        together([zs[0][level - 1], zs[1][level - 1]], prepare_next, updates)
        piv_row += held

    spare = b_v.reshape(SB * B, N)
    for gather in gathers:
        gather.drain(spare)
    for copy in stores:
        copy.wait()


def tables(sub_pattern, sub_map, front_map):
    leaf = lax.axis_index("leaf")
    front = lax.axis_index("front")
    pivots = jnp.arange(PB, dtype=jnp.int32)
    places, flags = [], []
    maps = lax.dynamic_slice_in_dim(sub_map, leaf * 8, 8)
    wanted = jnp.concatenate([pivots, PB + 2 * front + jnp.arange(2, dtype=jnp.int32)])
    match = maps[None] == wanted[:, None, None]
    places.append(2 * jnp.arange(8, dtype=jnp.int32) + match[:, :, 1].astype(jnp.int32))
    flags.append(match.any(axis=2))
    for level in range(2, LEVELS + 1):
        held = HELD[level - 1]
        maps = lax.dynamic_slice_in_dim(
            front_map, MAP_AT[level - 2] + 2 * (leaf // 2 ** (level - 1)), 2
        )
        row = ((leaf % 2 ** (level - 1)) * 8 + front) * held
        wanted = jnp.concatenate([pivots, (PB + row // B)[None]])
        match = maps[None] == wanted[:, None, None]
        place = jnp.sum(match * jnp.arange(PB, dtype=jnp.int32), axis=2, dtype=jnp.int32)
        place = place + jnp.array([0, PB], jnp.int32)
        last = jnp.arange(PB + 1)[:, None] == PB
        unit = min(B, 2 * held)
        place = jnp.where(last, place * (B // unit) + row % B // unit, place)
        places.append(jnp.pad(place, ((0, 0), (0, 6))))
        flags.append(jnp.pad(match.any(axis=2), ((0, 0), (0, 6))))
    found = jnp.concatenate([jnp.concatenate(places), jnp.concatenate(flags).astype(jnp.int32)], axis=1)
    return jnp.concatenate([found, jnp.pad(sub_pattern[:, 1:], ((0, 0), (0, 15)))])


def per_device(
    sub_rhs, sub_dinv, sub_off, sub_pattern, sub_update, sub_map,
    front_rhs, piv_inverse, upd_factor, front_map,
):
    def wide(level, held):
        return pltpu.VMEM((YS[level - 1], ZS[level - 1], 4, 2, held, N), F32)

    scratch = [
        pltpu.VMEM((SB, B, N), F32),
        pltpu.VMEM((SB, B, B), F32),
        pltpu.VMEM((SB - 1, K, B, B), F32),
        pltpu.VMEM((2 * B, SB * B), F32),
        pltpu.VMEM((PROWS, ROWS), F32),
        pltpu.VMEM((UROWS, ROWS), F32),
        pltpu.VMEM((SB, B, N), F32),
        pltpu.VMEM((SB, B, 2 * N), BF16),
        pltpu.VMEM((2, 2 * B, 2 * B), BF16),
        pltpu.VMEM((2, B, N), F32),
        pltpu.VMEM((2 * B, N), F32),
        pltpu.VMEM((2, ROWS // 2, N), F32),
        pltpu.VMEM((ROWS, N), BF16),
        pltpu.VMEM((2 * PROWS, ROWS), BF16),
        pltpu.VMEM((2 * UROWS, ROWS), BF16),
        pltpu.VMEM((PROWS, N), F32),
    ]
    scratch += [wide(level, HELD[level - 1]) for level in range(1, 6)]
    for _ in range(2):
        scratch += [wide(1, B)]
        scratch += [wide(level + 1, HELD[level - 1] // 2) for level in range(1, 5)]
        scratch += [wide(level, HELD[level - 1] // 2) for level in range(1, 5)]
    copies = 3 * sum(SENDS) + 2 * sum(SENDS[:4]) + 23
    scratch += [
        pltpu.SemaphoreType.DMA((15,)),
        pltpu.SemaphoreType.DMA((6,)),
        pltpu.SemaphoreType.DMA((23,)),
        pltpu.SemaphoreType.DMA((copies,)),
    ]
    smem = pl.BlockSpec(memory_space=pltpu.SMEM)
    hbm = pl.BlockSpec(memory_space=pl.ANY)
    solved, fronts = pl.pallas_call(
        kernel,
        out_shape=(
            jax.ShapeDtypeStruct((SB, B, N), F32),
            jax.ShapeDtypeStruct((PROWS, N), F32),
        ),
        in_specs=[smem] + [hbm] * 7,
        out_specs=(hbm, hbm),
        scratch_shapes=scratch,
        compiler_params=pltpu.CompilerParams(
            collective_id=0, has_side_effects=True, vmem_limit_bytes=62 * 2**20
        ),
    )(
        tables(sub_pattern, sub_map, front_map),
        sub_rhs.reshape(SB, B, N), sub_dinv, sub_off, sub_update, front_rhs, piv_inverse, upd_factor,
    )
    return solved.reshape(SB * B, N), fronts


def solution(mesh):
    rows = P(("leaf", "front"), None)
    return jax.shard_map(
        per_device,
        mesh=mesh,
        in_specs=(
            rows,
            P(("leaf", "front"), None, None),
            P(("leaf", "front"), None, None, None),
            rows,
            rows,
            P(),
            rows,
            rows,
            rows,
            P(),
        ),
        out_specs=(rows, rows),
        check_vma=False,
    )
```

```python
import itertools

import jax
import jax.numpy as jnp
from jax import lax
from jax.experimental import pallas as pl
from jax.experimental.pallas import tpu as pltpu
from jax.sharding import PartitionSpec as P

B = 128
N = 128
SB = 24
K = 2
ROWS = 2048
PB = 16
LEVELS = 5
PROWS = 496
UROWS = 480
MAPROWS = 30
YS = (1, 1, 1, 2, 4)
ZS = (1, 2, 4, 4, 4)
HELD = (256, 128, 64, 32, 16)
MAP_AT = (0, 16, 24, 28)
ENTRY_AT = (None, 0, 18, 35, 52, 69)
MIXED = (("x", "zy"), ("zy", "x"))
SAME = (("x", "zy"), ("x", "zy"))
SENDS = (3, 7, 15, 10, 18)
HALF = 64
COLUMNS_AT = 86
EARLY = 8
F32 = jnp.float32
BF16 = jnp.bfloat16


def split(value):
    high = value.astype(BF16)
    return high, (value - high.astype(F32)).astype(BF16)


def side(value):
    return jnp.concatenate(split(value), axis=1)


def stack(value):
    return jnp.concatenate(split(value), axis=0)


def dot(left, right):
    return jnp.dot(left, right, preferred_element_type=F32)


def fold(product):
    half = product.shape[0] // 2
    return product[:half, :N] + (product[:half, N:] + product[half:, :N])


def low_half(shape):
    return lax.broadcasted_iota(jnp.int32, shape, len(shape) - 1) < HALF


def turned(value):
    return pltpu.roll(value, HALF, 1)


def choose(low, high):
    return jnp.where(low_half(low.shape), low, high)


def pairs(value, unit):
    many = value.shape[0]
    blocks = value.reshape(many // unit, unit, N)
    shape = (many // 2, N)
    return blocks[:, : unit // 2].reshape(shape), blocks[:, unit // 2 :].reshape(shape)


def streams_of(value, unit):
    lower, upper = pairs(value, unit)
    return choose(lower, turned(upper)), choose(turned(lower), upper)


def pack(value, unit):
    return choose(*pairs(value, unit))


def operand(packed, unit):
    high = packed.astype(BF16).astype(F32)
    low = turned(packed - high)
    shape = (2 * packed.shape[0] // unit, unit // 2, N)
    pair = [choose(high, low).reshape(shape), choose(low, high).reshape(shape)]
    return jnp.concatenate(pair, axis=1).reshape(2 * packed.shape[0], N).astype(BF16)


def fold_both(product):
    half = product.shape[0] // 2
    total = product[:half] + product[half:]
    return total + turned(total)


class Gather:
    def __init__(self, buf, send, recv, level, at, order):
        self.buf, self.send, self.recv, self.at = buf, send, recv, at
        self.level, eager = level, level < 4
        self.size = {"x": 4, "z": ZS[level - 1], "y": YS[level - 1]}
        self.order, self.eager = order, eager
        self.own = {d: 0 if self.size[d] == 1 else at[d] % self.size[d] for d in "yzx"}

    def sets(self, core):
        found = ["".join(d for d in dims if self.size[d] > 1) for dims in self.order[core]]
        return found[0] or found[1], found[1] if found[0] else ""

    def hops(self, dims):
        steps = [
            dict(zip(dims, offsets))
            for offsets in itertools.product(*(range(self.size[d]) for d in dims))
            if any(offsets)
        ]
        return sorted(steps, key=lambda step: sum(min(o, self.size[d] - o) for d, o in step.items()))

    def moved(self, dim, offset):
        here = self.at[dim]
        if offset == 0:
            return here
        if self.size[dim] == 4:
            return (here + offset) % 4
        return here + 1 - 2 * (here % 2)

    def origin(self, step):
        return {
            d: self.moved(d, -o % self.size[d]) % self.size[d] for d, o in step.items()
        }

    def view(self, core, full="", **places):
        place = {**self.own, **places}
        index = [slice(None) if d in full else place[d] for d in "yzx"]
        return self.buf.at[index[0], index[1], index[2], core]

    def copy(self, view, which, **changes):
        place = {**self.at, **changes}
        return pltpu.make_async_remote_copy(
            src_ref=view,
            dst_ref=view,
            send_sem=self.send,
            recv_sem=self.recv.at[which],
            device_id=(place["y"] * 4 + place["z"], place["x"] * 2 + place["core"]),
            device_id_type=pl.DeviceIdType.MESH,
        )

    def to(self, step):
        return {d: self.moved(d, o) for d, o in step.items()}

    def out(self, view, which, core, step):
        return lambda: self.copy(view, which, core=core, **self.to(step))

    def across(self, view, which, core):
        return lambda: self.copy(view, which, core=1 - core)

    def plan(self, core):
        first, second = self.sets(core)
        near, far = self.hops(first), self.hops(second) if second else []
        cross = SENDS[self.level - 1]
        begin = [self.out(self.view(core), i, core, step) for i, step in enumerate(near)]
        used = len(near)
        middle, close = [], []
        held = [{}] + [self.origin(step) for step in near]
        sets = [held[i : i + 1] for i in range(len(held))] if self.eager else [held]
        sends = []
        for group in sets:
            view = self.view(core, **group[0]) if self.eager else self.view(core, first)
            sends.append([self.out(view, used + j, core, step) for j, step in enumerate(far)])
            used += len(far)
        if self.eager:
            begin += sends[0]
        for i, step in enumerate(near):
            view = self.view(core, **held[i + 1])
            after = sends[i + 1] if self.eager else sends[0] if i == len(near) - 1 else []
            middle.append(([(view, i)], after + [self.across(view, cross, core)]))
        if not second:
            middle = [(wait, [start[-1]]) for wait, start in middle]
        for j, step in enumerate(far):
            origin = self.origin(step)
            waits = []
            for g, group in enumerate(sets):
                if self.eager:
                    view = self.view(core, **{**group[0], **origin})
                else:
                    view = self.view(core, first, **origin)
                waits.append((view, len(near) + g * len(far) + j))
            view = self.view(core, first, **origin)
            close.append((waits, [self.across(view, cross, core)]))
        begin.append(self.across(self.view(core), cross, core))
        return begin, middle, close

    def begin(self, core):
        for make in self.plan(core)[0]:
            make().start()

    def follow(self, steps, core):
        for waits, starts in steps:
            for view, which in waits:
                self.copy(view, which, core=1 - core).wait_recv()
            for make in starts:
                make().start()

    def middle(self, core):
        self.follow(self.plan(core)[1], core)

    def close(self, core):
        self.follow(self.plan(core)[2], core)

    def finish(self, core):
        half = self.view(1 - core, "yzx")
        self.copy(half, SENDS[self.level - 1], core=1 - core).wait_recv()

    def drain(self, spare):
        rows = (8 * self.size["y"] * self.size["z"] - 1) * self.buf.shape[-2]
        view = spare.at[pl.ds(0, rows)]
        self.copy(view, 0, core=1 - self.at["core"]).wait_send()


def kernel(
    table,
    rhs, dinv, off, update, front_rhs, piv, factor,
    solved_out, front_out,
    b_v, d_v, l_v, u_v, m_v, e_v, y_v, yhl_v, g_v, c_v, acc_v, p_v, rhs_v, ms_v, es_v, z_v,
    h1, h2, h3, h4, h5, *rest,
):
    leaf = lax.axis_index("leaf")
    front = lax.axis_index("front")
    core = front % 2
    at = {"y": leaf // 4, "z": leaf % 4, "x": front // 2, "core": core}

    def both(step):
        for which in (0, 1):
            @pl.when(core == which)
            def _():
                step(which)

    streams, (load_sem, store_sem, send, recv) = rest[:18], rest[18:]
    levels = [1, 2, 3, 4, 5] + 2 * [1, 2, 3, 4, 5, 1, 2, 3, 4]
    gathers = []
    base = 0
    for buf, level in zip((h1, h2, h3, h4, h5, *streams), levels):
        order = SAME if len(gathers) < 5 else MIXED
        copies = SENDS[level - 1] + 1
        gathers.append(
            Gather(buf, send.at[len(gathers)], recv.at[pl.ds(base, copies)], level, at, order)
        )
        base += copies
    hs = gathers[:5]
    ws = (gathers[5:10], gathers[14:19])
    zs = (gathers[10:14], gathers[19:23])

    def mine(gather):
        own = gather.own
        return (own["y"], own["z"], own["x"], core)

    loads = []

    def load(source, target):
        copy = pltpu.make_async_copy(source, target, load_sem.at[len(loads)])
        copy.start()
        loads.append(copy)

    row = 0
    for gather, held in zip(hs, HELD):
        load(front_rhs.at[pl.ds(row, held)], gather.buf.at[mine(gather)])
        row += held
    for first, many in ((0, EARLY), (EARLY, SB - EARLY)):
        load(dinv.at[pl.ds(first, many)], d_v.at[pl.ds(first, many)])
        load(off.at[pl.ds(first, many - first // EARLY)], l_v.at[pl.ds(first, many - first // EARLY)])
        load(rhs.at[pl.ds(first, many)], b_v.at[pl.ds(first, many)])
        columns = pl.ds(first * B, many * B)
        load(update.at[:, columns], u_v.at[:, columns])
    load(piv, m_v)
    load(factor, e_v)

    barrier = pltpu.get_barrier_semaphore()
    peers = [(at["y"], at["z"], (at["x"] + o) % 4, core) for o in (1, 2, 3)]
    peers += [
        ((at["y"] + oy) % 4, (at["z"] + oz) % 4, at["x"], core)
        for oy in range(4)
        for oz in range(4)
        if oy or oz
    ]
    peers.append((at["y"], at["z"], at["x"], 1 - core))
    for y, z, x, c in peers:
        pl.semaphore_signal(
            barrier, inc=1, device_id=(y * 4 + z, x * 2 + c), device_id_type=pl.DeviceIdType.MESH
        )
    pl.semaphore_wait(barrier, len(peers))

    for copy in loads[:5]:
        copy.wait()
    both(lambda c: [gather.begin(c) for gather in hs])
    for copy in loads[5:9]:
        copy.wait()

    def prepare(block, slot):
        high, low = split(d_v[block])
        wide = jnp.concatenate([l_v[block - 1, 0], l_v[block - 1, 1], b_v[block]], axis=1)
        wide_high, wide_low = split(wide)
        first = dot(jnp.concatenate([high, low], axis=0), wide_high)
        product = first[:B] + (first[B:] + dot(high, wide_low))
        g_v[slot] = stack(product[:, : 2 * B])
        c_v[slot] = product[:, 2 * B :]

    def keep(block, value):
        y_v[block] = value
        yhl_v[block] = side(value)

    def couple(block):
        columns = pl.ds(pl.multiple_of(block * B, B), B)
        acc_v[...] += fold(dot(stack(u_v[:, columns]), yhl_v[block]))

    keep(0, fold(dot(stack(d_v[0]), side(b_v[0]))))
    prepare(1, 1)
    acc_v[...] = jnp.zeros_like(acc_v)

    def advance(block, carry):
        slot = lax.rem(block, 2)
        known = jnp.concatenate([yhl_v[block - 1], yhl_v[table[COLUMNS_AT + block - 1, 0]]], axis=0)
        value = c_v[slot] - fold(dot(g_v[slot], known))
        couple(block - 1)
        prepare(jnp.minimum(block + 1, SB - 1), 1 - slot)
        keep(block, value)
        return carry

    lax.fori_loop(1, EARLY - 1, advance, 0)
    for copy in loads[9:13]:
        copy.wait()
    lax.fori_loop(EARLY - 1, SB, advance, 0)
    couple(SB - 1)

    stores = []

    def store(source, target):
        copy = pltpu.make_async_copy(source, target, store_sem.at[len(stores)])
        copy.start()
        stores.append(copy)

    def widen(source, target, row, held):
        tall = min(held, B)
        for first in range(row, row + held, tall):
            target[2 * first : 2 * (first + tall), :] = stack(source[first : first + tall, :])

    def unit_of(level):
        return B if level == 1 else min(B, HELD[level - 2])

    def fill(level):
        gather = hs[level - 1]

        both(gather.finish)
        held = HELD[level - 1]
        many = 8 * held
        for y in range(YS[level - 1]):
            for z in range(ZS[level - 1]):
                first = (y * ZS[level - 1] + z) * many
                rows = slice(first // 2, (first + many) // 2)
                parts = streams_of(gather.buf[y, z].reshape(many, N), unit_of(level))
                p_v[0, rows, :], p_v[1, rows, :] = parts

    def send_update(stream, level, value):
        gather = ws[stream][level]
        own = mine(gather)
        gather.buf[own] = value
        both(gather.begin)

    def hit(entry, which):
        return table[entry, 8 + which].astype(F32)

    def landed(stream, level, entry):
        gather = ws[stream][level - 1]
        blocks = gather.buf.reshape(PB if level == 1 else 2 * PB, HALF, N)
        total = hit(entry, 0) * blocks[table[entry, 0]]
        for child in range(1, 8 if level == 1 else 2):
            total = total + hit(entry, child) * blocks[table[entry, child]]
        return total

    def place(stream, level):
        def body(block, carry):
            packed = pl.ds(pl.multiple_of(block * HALF, HALF), HALF)
            rows = pl.ds(pl.multiple_of(block * B, B), B)
            total = p_v[stream, packed, :] + landed(stream, level, ENTRY_AT[level] + block)
            rhs_v[rows, :] = operand(total, unit_of(level))
            return carry

        lax.fori_loop(0, PB, body, 0, unroll=8)

    def update_rows(stream, level):
        entry = ENTRY_AT[level] + PB
        if level == 1:
            return jnp.concatenate([landed(stream, 1, entry + i) for i in (0, 1)], axis=0)
        if level == 2:
            return landed(stream, 2, entry)
        held = HELD[level - 1]
        pieces = ws[stream][level - 1].buf.reshape(ROWS // held, held, N)
        total = (
            hit(entry, 0) * pieces[table[entry, 0]] + hit(entry, 1) * pieces[table[entry, 1]]
        )
        lower, upper = pairs(jnp.where(core == 0, total, turned(total)), held)
        return choose(lower, turned(upper))

    def multiply(matrix, row, held, chunks):
        tall = min(held, B)
        totals = []
        for first in range(row, row + held, tall):
            total = None
            column = 0
            for right in chunks:
                depth = right.shape[0]
                left = matrix[2 * first : 2 * (first + tall), column : column + depth]
                part = dot(left, right)
                total = part if total is None else total + part
                column += depth
            totals.append(fold_both(total))
        return totals[0] if len(totals) == 1 else jnp.concatenate(totals, axis=0)

    def together(pair, before, after):
        before()

        def start(c):
            for gather in pair:
                gather.middle(c)

        both(start)
        for stream, gather in enumerate(pair):

            def rest(c, gather=gather):
                gather.close(c)
                gather.finish(c)

            both(rest)
            after(stream)

    for stream, value in enumerate(streams_of(-acc_v[...], B)):
        send_update(stream, 0, value)

    def before_first():
        both(lambda c: [gather.middle(c) for gather in hs])
        store(y_v, solved_out)
        fill(1)
        loads[13].wait()
        widen(m_v, ms_v, 0, HELD[0])
        loads[14].wait()
        widen(e_v, es_v, 0, HELD[0])

    piv_row = 0
    for level in range(1, LEVELS + 1):
        held = HELD[level - 1]
        rows = pl.ds(piv_row, held)
        last = level == LEVELS

        def before_pivots(level=level):
            if level < LEVELS:
                both(hs[level].close)

        def pivots(stream, level=level, row=piv_row, held=held, last=last):
            place(stream, level)
            value = multiply(ms_v, row, held, [rhs_v[...]])
            if not last:
                gather = zs[stream][level - 1]
                own = mine(gather)
                gather.buf[own] = pack(value, min(held, B))
                both(gather.begin)
            if level == 1 and stream == 0:
                both(hs[1].close)
            if stream == 0:
                z_v[row : row + held, :] = value
            else:
                z_v[row : row + held, :] = choose(z_v[row : row + held, :], value)

        together([ws[0][level - 1], ws[1][level - 1]], before_first if level == 1 else before_pivots, pivots)
        store(z_v.at[rows], front_out.at[rows])
        if last:
            break

        def prepare_next(level=level, row=piv_row, held=held):
            widen(m_v, ms_v, row + held, HELD[level])
            if level + 1 < LEVELS:
                widen(e_v, es_v, row + held, HELD[level])
            fill(level + 1)

        def updates(stream, level=level, row=piv_row, held=held):
            gather = zs[stream][level - 1]
            chunks = [
                operand(gather.buf[y, z].reshape(4 * held, N), min(held, B))
                for y in range(YS[level - 1])
                for z in range(ZS[level - 1])
            ]
            value = pack(multiply(es_v, row, held, chunks), min(held, B))
            send_update(stream, level, update_rows(stream, level) - value)

        together([zs[0][level - 1], zs[1][level - 1]], prepare_next, updates)
        piv_row += held

    spare = b_v.reshape(SB * B, N)
    for gather in gathers:
        gather.drain(spare)
    for copy in stores:
        copy.wait()


def tables(sub_pattern, sub_map, front_map):
    leaf = lax.axis_index("leaf")
    front = lax.axis_index("front")
    pivots = jnp.arange(PB, dtype=jnp.int32)
    places, flags = [], []
    maps = lax.dynamic_slice_in_dim(sub_map, leaf * 8, 8)
    wanted = jnp.concatenate([pivots, PB + 2 * front + jnp.arange(2, dtype=jnp.int32)])
    match = maps[None] == wanted[:, None, None]
    places.append(2 * jnp.arange(8, dtype=jnp.int32) + match[:, :, 1].astype(jnp.int32))
    flags.append(match.any(axis=2))
    for level in range(2, LEVELS + 1):
        held = HELD[level - 1]
        maps = lax.dynamic_slice_in_dim(
            front_map, MAP_AT[level - 2] + 2 * (leaf // 2 ** (level - 1)), 2
        )
        row = ((leaf % 2 ** (level - 1)) * 8 + front) * held
        wanted = jnp.concatenate([pivots, (PB + row // B)[None]])
        match = maps[None] == wanted[:, None, None]
        place = jnp.sum(match * jnp.arange(PB, dtype=jnp.int32), axis=2, dtype=jnp.int32)
        place = place + jnp.array([0, PB], jnp.int32)
        last = jnp.arange(PB + 1)[:, None] == PB
        unit = min(B, 2 * held)
        place = jnp.where(last, place * (B // unit) + row % B // unit, place)
        places.append(jnp.pad(place, ((0, 0), (0, 6))))
        flags.append(jnp.pad(match.any(axis=2), ((0, 0), (0, 6))))
    found = jnp.concatenate([jnp.concatenate(places), jnp.concatenate(flags).astype(jnp.int32)], axis=1)
    return jnp.concatenate([found, jnp.pad(sub_pattern[:, 1:], ((0, 0), (0, 15)))])


def per_device(
    sub_rhs, sub_dinv, sub_off, sub_pattern, sub_update, sub_map,
    front_rhs, piv_inverse, upd_factor, front_map,
):
    def wide(level, held):
        return pltpu.VMEM((YS[level - 1], ZS[level - 1], 4, 2, held, N), F32)

    scratch = [
        pltpu.VMEM((SB, B, N), F32),
        pltpu.VMEM((SB, B, B), F32),
        pltpu.VMEM((SB - 1, K, B, B), F32),
        pltpu.VMEM((2 * B, SB * B), F32),
        pltpu.VMEM((PROWS, ROWS), F32),
        pltpu.VMEM((UROWS, ROWS), F32),
        pltpu.VMEM((SB, B, N), F32),
        pltpu.VMEM((SB, B, 2 * N), BF16),
        pltpu.VMEM((2, 2 * B, 2 * B), BF16),
        pltpu.VMEM((2, B, N), F32),
        pltpu.VMEM((2 * B, N), F32),
        pltpu.VMEM((2, ROWS // 2, N), F32),
        pltpu.VMEM((ROWS, N), BF16),
        pltpu.VMEM((2 * PROWS, ROWS), BF16),
        pltpu.VMEM((2 * UROWS, ROWS), BF16),
        pltpu.VMEM((PROWS, N), F32),
    ]
    scratch += [wide(level, HELD[level - 1]) for level in range(1, 6)]
    for _ in range(2):
        scratch += [wide(1, B)]
        scratch += [wide(level + 1, HELD[level - 1] // 2) for level in range(1, 5)]
        scratch += [wide(level, HELD[level - 1] // 2) for level in range(1, 5)]
    copies = 3 * sum(SENDS) + 2 * sum(SENDS[:4]) + 23
    scratch += [
        pltpu.SemaphoreType.DMA((15,)),
        pltpu.SemaphoreType.DMA((6,)),
        pltpu.SemaphoreType.DMA((23,)),
        pltpu.SemaphoreType.DMA((copies,)),
    ]
    smem = pl.BlockSpec(memory_space=pltpu.SMEM)
    hbm = pl.BlockSpec(memory_space=pl.ANY)
    solved, fronts = pl.pallas_call(
        kernel,
        out_shape=(
            jax.ShapeDtypeStruct((SB, B, N), F32),
            jax.ShapeDtypeStruct((PROWS, N), F32),
        ),
        in_specs=[smem] + [hbm] * 7,
        out_specs=(hbm, hbm),
        scratch_shapes=scratch,
        compiler_params=pltpu.CompilerParams(
            collective_id=0, has_side_effects=True, vmem_limit_bytes=62 * 2**20
        ),
    )(
        tables(sub_pattern, sub_map, front_map),
        sub_rhs.reshape(SB, B, N), sub_dinv, sub_off, sub_update, front_rhs, piv_inverse, upd_factor,
    )
    return solved.reshape(SB * B, N), fronts


def solution(mesh):
    rows = P(("leaf", "front"), None)
    return jax.shard_map(
        per_device,
        mesh=mesh,
        in_specs=(
            rows,
            P(("leaf", "front"), None, None),
            P(("leaf", "front"), None, None, None),
            rows,
            rows,
            P(),
            rows,
            rows,
            rows,
            P(),
        ),
        out_specs=(rows, rows),
        check_vma=False,
    )
```

```python
import itertools

import jax
import jax.numpy as jnp
from jax import lax
from jax.experimental import pallas as pl
from jax.experimental.pallas import tpu as pltpu
from jax.sharding import PartitionSpec as P

B = 128
N = 128
SB = 24
K = 2
ROWS = 2048
PB = 16
LEVELS = 5
PROWS = 496
UROWS = 480
MAPROWS = 30
YS = (1, 1, 1, 2, 4)
ZS = (1, 2, 4, 4, 4)
HELD = (256, 128, 64, 32, 16)
MAP_AT = (0, 16, 24, 28)
ENTRY_AT = (None, 0, 18, 35, 52, 69)
MIXED = (("x", "zy"), ("zy", "x"))
SAME = (("x", "zy"), ("x", "zy"))
SENDS = (3, 7, 15, 10, 18)
HALF = 64
COLUMNS_AT = 86
EARLY = 9
F32 = jnp.float32
BF16 = jnp.bfloat16


def split(value):
    high = value.astype(BF16)
    return high, (value - high.astype(F32)).astype(BF16)


def side(value):
    return jnp.concatenate(split(value), axis=1)


def stack(value):
    return jnp.concatenate(split(value), axis=0)


def dot(left, right):
    return jnp.dot(left, right, preferred_element_type=F32)


def fold(product):
    half = product.shape[0] // 2
    return product[:half, :N] + (product[:half, N:] + product[half:, :N])


def low_half(shape):
    return lax.broadcasted_iota(jnp.int32, shape, len(shape) - 1) < HALF


def turned(value):
    return pltpu.roll(value, HALF, 1)


def choose(low, high):
    return jnp.where(low_half(low.shape), low, high)


def pairs(value, unit):
    many = value.shape[0]
    blocks = value.reshape(many // unit, unit, N)
    shape = (many // 2, N)
    return blocks[:, : unit // 2].reshape(shape), blocks[:, unit // 2 :].reshape(shape)


def streams_of(value, unit):
    lower, upper = pairs(value, unit)
    return choose(lower, turned(upper)), choose(turned(lower), upper)


def pack(value, unit):
    return choose(*pairs(value, unit))


def operand(packed, unit):
    high = packed.astype(BF16).astype(F32)
    low = turned(packed - high)
    shape = (2 * packed.shape[0] // unit, unit // 2, N)
    pair = [choose(high, low).reshape(shape), choose(low, high).reshape(shape)]
    return jnp.concatenate(pair, axis=1).reshape(2 * packed.shape[0], N).astype(BF16)


def fold_both(product):
    half = product.shape[0] // 2
    total = product[:half] + product[half:]
    return total + turned(total)


class Gather:
    def __init__(self, buf, send, recv, level, at, order):
        self.buf, self.send, self.recv, self.at = buf, send, recv, at
        self.level, eager = level, level < 4
        self.size = {"x": 4, "z": ZS[level - 1], "y": YS[level - 1]}
        self.order, self.eager = order, eager
        self.own = {d: 0 if self.size[d] == 1 else at[d] % self.size[d] for d in "yzx"}

    def sets(self, core):
        found = ["".join(d for d in dims if self.size[d] > 1) for dims in self.order[core]]
        return found[0] or found[1], found[1] if found[0] else ""

    def hops(self, dims):
        steps = [
            dict(zip(dims, offsets))
            for offsets in itertools.product(*(range(self.size[d]) for d in dims))
            if any(offsets)
        ]
        return sorted(steps, key=lambda step: sum(min(o, self.size[d] - o) for d, o in step.items()))

    def moved(self, dim, offset):
        here = self.at[dim]
        if offset == 0:
            return here
        if self.size[dim] == 4:
            return (here + offset) % 4
        return here + 1 - 2 * (here % 2)

    def origin(self, step):
        return {
            d: self.moved(d, -o % self.size[d]) % self.size[d] for d, o in step.items()
        }

    def view(self, core, full="", **places):
        place = {**self.own, **places}
        index = [slice(None) if d in full else place[d] for d in "yzx"]
        return self.buf.at[index[0], index[1], index[2], core]

    def copy(self, view, which, **changes):
        place = {**self.at, **changes}
        return pltpu.make_async_remote_copy(
            src_ref=view,
            dst_ref=view,
            send_sem=self.send,
            recv_sem=self.recv.at[which],
            device_id=(place["y"] * 4 + place["z"], place["x"] * 2 + place["core"]),
            device_id_type=pl.DeviceIdType.MESH,
        )

    def to(self, step):
        return {d: self.moved(d, o) for d, o in step.items()}

    def out(self, view, which, core, step):
        return lambda: self.copy(view, which, core=core, **self.to(step))

    def across(self, view, which, core):
        return lambda: self.copy(view, which, core=1 - core)

    def plan(self, core):
        first, second = self.sets(core)
        near, far = self.hops(first), self.hops(second) if second else []
        cross = SENDS[self.level - 1]
        begin = [self.out(self.view(core), i, core, step) for i, step in enumerate(near)]
        used = len(near)
        middle, close = [], []
        held = [{}] + [self.origin(step) for step in near]
        sets = [held[i : i + 1] for i in range(len(held))] if self.eager else [held]
        sends = []
        for group in sets:
            view = self.view(core, **group[0]) if self.eager else self.view(core, first)
            sends.append([self.out(view, used + j, core, step) for j, step in enumerate(far)])
            used += len(far)
        if self.eager:
            begin += sends[0]
        for i, step in enumerate(near):
            view = self.view(core, **held[i + 1])
            after = sends[i + 1] if self.eager else sends[0] if i == len(near) - 1 else []
            middle.append(([(view, i)], after + [self.across(view, cross, core)]))
        if not second:
            middle = [(wait, [start[-1]]) for wait, start in middle]
        for j, step in enumerate(far):
            origin = self.origin(step)
            waits = []
            for g, group in enumerate(sets):
                if self.eager:
                    view = self.view(core, **{**group[0], **origin})
                else:
                    view = self.view(core, first, **origin)
                waits.append((view, len(near) + g * len(far) + j))
            view = self.view(core, first, **origin)
            close.append((waits, [self.across(view, cross, core)]))
        begin.append(self.across(self.view(core), cross, core))
        return begin, middle, close

    def begin(self, core):
        for make in self.plan(core)[0]:
            make().start()

    def follow(self, steps, core):
        for waits, starts in steps:
            for view, which in waits:
                self.copy(view, which, core=1 - core).wait_recv()
            for make in starts:
                make().start()

    def middle(self, core):
        self.follow(self.plan(core)[1], core)

    def close(self, core):
        self.follow(self.plan(core)[2], core)

    def finish(self, core):
        half = self.view(1 - core, "yzx")
        self.copy(half, SENDS[self.level - 1], core=1 - core).wait_recv()

    def drain(self, spare):
        rows = (8 * self.size["y"] * self.size["z"] - 1) * self.buf.shape[-2]
        view = spare.at[pl.ds(0, rows)]
        self.copy(view, 0, core=1 - self.at["core"]).wait_send()


def kernel(
    table,
    rhs, dinv, off, update, front_rhs, piv, factor,
    solved_out, front_out,
    b_v, d_v, l_v, u_v, m_v, e_v, y_v, yhl_v, g_v, c_v, acc_v, p_v, rhs_v, ms_v, es_v, z_v,
    h1, h2, h3, h4, h5, *rest,
):
    leaf = lax.axis_index("leaf")
    front = lax.axis_index("front")
    core = front % 2
    at = {"y": leaf // 4, "z": leaf % 4, "x": front // 2, "core": core}

    def both(step):
        for which in (0, 1):
            @pl.when(core == which)
            def _():
                step(which)

    streams, (load_sem, store_sem, send, recv) = rest[:18], rest[18:]
    levels = [1, 2, 3, 4, 5] + 2 * [1, 2, 3, 4, 5, 1, 2, 3, 4]
    gathers = []
    base = 0
    for buf, level in zip((h1, h2, h3, h4, h5, *streams), levels):
        order = SAME if len(gathers) < 5 else MIXED
        copies = SENDS[level - 1] + 1
        gathers.append(
            Gather(buf, send.at[len(gathers)], recv.at[pl.ds(base, copies)], level, at, order)
        )
        base += copies
    hs = gathers[:5]
    ws = (gathers[5:10], gathers[14:19])
    zs = (gathers[10:14], gathers[19:23])

    def mine(gather):
        own = gather.own
        return (own["y"], own["z"], own["x"], core)

    loads = []

    def load(source, target):
        copy = pltpu.make_async_copy(source, target, load_sem.at[len(loads)])
        copy.start()
        loads.append(copy)

    row = 0
    for gather, held in zip(hs, HELD):
        load(front_rhs.at[pl.ds(row, held)], gather.buf.at[mine(gather)])
        row += held
    for first, many in ((0, EARLY), (EARLY, SB - EARLY)):
        load(dinv.at[pl.ds(first, many)], d_v.at[pl.ds(first, many)])
        load(off.at[pl.ds(first, many - first // EARLY)], l_v.at[pl.ds(first, many - first // EARLY)])
        load(rhs.at[pl.ds(first, many)], b_v.at[pl.ds(first, many)])
        columns = pl.ds(first * B, many * B)
        load(update.at[:, columns], u_v.at[:, columns])
    load(piv, m_v)
    load(factor, e_v)

    barrier = pltpu.get_barrier_semaphore()
    peers = [(at["y"], at["z"], (at["x"] + o) % 4, core) for o in (1, 2, 3)]
    peers += [
        ((at["y"] + oy) % 4, (at["z"] + oz) % 4, at["x"], core)
        for oy in range(4)
        for oz in range(4)
        if oy or oz
    ]
    peers.append((at["y"], at["z"], at["x"], 1 - core))
    for y, z, x, c in peers:
        pl.semaphore_signal(
            barrier, inc=1, device_id=(y * 4 + z, x * 2 + c), device_id_type=pl.DeviceIdType.MESH
        )
    pl.semaphore_wait(barrier, len(peers))

    for copy in loads[:5]:
        copy.wait()
    both(lambda c: [gather.begin(c) for gather in hs])
    for copy in loads[5:9]:
        copy.wait()

    def prepare(block, slot):
        high, low = split(d_v[block])
        wide = jnp.concatenate([l_v[block - 1, 0], l_v[block - 1, 1], b_v[block]], axis=1)
        wide_high, wide_low = split(wide)
        first = dot(jnp.concatenate([high, low], axis=0), wide_high)
        product = first[:B] + (first[B:] + dot(high, wide_low))
        g_v[slot] = stack(product[:, : 2 * B])
        c_v[slot] = product[:, 2 * B :]

    def keep(block, value):
        y_v[block] = value
        yhl_v[block] = side(value)

    def couple(block):
        columns = pl.ds(pl.multiple_of(block * B, B), B)
        acc_v[...] += fold(dot(stack(u_v[:, columns]), yhl_v[block]))

    keep(0, fold(dot(stack(d_v[0]), side(b_v[0]))))
    prepare(1, 1)
    acc_v[...] = jnp.zeros_like(acc_v)

    def advance(block, carry):
        slot = lax.rem(block, 2)
        known = jnp.concatenate([yhl_v[block - 1], yhl_v[table[COLUMNS_AT + block - 1, 0]]], axis=0)
        value = c_v[slot] - fold(dot(g_v[slot], known))
        couple(block - 1)
        prepare(jnp.minimum(block + 1, SB - 1), 1 - slot)
        keep(block, value)
        return carry

    lax.fori_loop(1, EARLY - 1, advance, 0)
    for copy in loads[9:13]:
        copy.wait()
    lax.fori_loop(EARLY - 1, SB, advance, 0, unroll=2)
    couple(SB - 1)

    stores = []

    def store(source, target):
        copy = pltpu.make_async_copy(source, target, store_sem.at[len(stores)])
        copy.start()
        stores.append(copy)

    def widen(source, target, row, held):
        tall = min(held, B)
        for first in range(row, row + held, tall):
            target[2 * first : 2 * (first + tall), :] = stack(source[first : first + tall, :])

    def unit_of(level):
        return B if level == 1 else min(B, HELD[level - 2])

    def fill(level):
        gather = hs[level - 1]

        both(gather.finish)
        held = HELD[level - 1]
        many = 8 * held
        for y in range(YS[level - 1]):
            for z in range(ZS[level - 1]):
                first = (y * ZS[level - 1] + z) * many
                rows = slice(first // 2, (first + many) // 2)
                parts = streams_of(gather.buf[y, z].reshape(many, N), unit_of(level))
                p_v[0, rows, :], p_v[1, rows, :] = parts

    def send_update(stream, level, value):
        gather = ws[stream][level]
        own = mine(gather)
        gather.buf[own] = value
        both(gather.begin)

    def hit(entry, which):
        return table[entry, 8 + which].astype(F32)

    def landed(stream, level, entry):
        gather = ws[stream][level - 1]
        blocks = gather.buf.reshape(PB if level == 1 else 2 * PB, HALF, N)
        total = hit(entry, 0) * blocks[table[entry, 0]]
        for child in range(1, 8 if level == 1 else 2):
            total = total + hit(entry, child) * blocks[table[entry, child]]
        return total

    def place(stream, level):
        def body(block, carry):
            packed = pl.ds(pl.multiple_of(block * HALF, HALF), HALF)
            rows = pl.ds(pl.multiple_of(block * B, B), B)
            total = p_v[stream, packed, :] + landed(stream, level, ENTRY_AT[level] + block)
            rhs_v[rows, :] = operand(total, unit_of(level))
            return carry

        lax.fori_loop(0, PB, body, 0, unroll=8)

    def update_rows(stream, level):
        entry = ENTRY_AT[level] + PB
        if level == 1:
            return jnp.concatenate([landed(stream, 1, entry + i) for i in (0, 1)], axis=0)
        if level == 2:
            return landed(stream, 2, entry)
        held = HELD[level - 1]
        pieces = ws[stream][level - 1].buf.reshape(ROWS // held, held, N)
        total = (
            hit(entry, 0) * pieces[table[entry, 0]] + hit(entry, 1) * pieces[table[entry, 1]]
        )
        lower, upper = pairs(jnp.where(core == 0, total, turned(total)), held)
        return choose(lower, turned(upper))

    def multiply(matrix, row, held, chunks):
        tall = min(held, B)
        totals = []
        for first in range(row, row + held, tall):
            total = None
            column = 0
            for right in chunks:
                depth = right.shape[0]
                left = matrix[2 * first : 2 * (first + tall), column : column + depth]
                part = dot(left, right)
                total = part if total is None else total + part
                column += depth
            totals.append(fold_both(total))
        return totals[0] if len(totals) == 1 else jnp.concatenate(totals, axis=0)

    def together(pair, before, after):
        before()

        def start(c):
            for gather in pair:
                gather.middle(c)

        both(start)
        for stream, gather in enumerate(pair):

            def rest(c, gather=gather):
                gather.close(c)
                gather.finish(c)

            both(rest)
            after(stream)

    for stream, value in enumerate(streams_of(-acc_v[...], B)):
        send_update(stream, 0, value)

    def before_first():
        both(lambda c: [gather.middle(c) for gather in hs])
        store(y_v, solved_out)
        fill(1)
        loads[13].wait()
        widen(m_v, ms_v, 0, HELD[0])
        loads[14].wait()
        widen(e_v, es_v, 0, HELD[0])

    piv_row = 0
    for level in range(1, LEVELS + 1):
        held = HELD[level - 1]
        rows = pl.ds(piv_row, held)
        last = level == LEVELS

        def before_pivots(level=level):
            if level < LEVELS:
                both(hs[level].close)

        def pivots(stream, level=level, row=piv_row, held=held, last=last):
            place(stream, level)
            value = multiply(ms_v, row, held, [rhs_v[...]])
            if not last:
                gather = zs[stream][level - 1]
                own = mine(gather)
                gather.buf[own] = pack(value, min(held, B))
                both(gather.begin)
            if level == 1 and stream == 0:
                both(hs[1].close)
            if stream == 0:
                z_v[row : row + held, :] = value
            else:
                z_v[row : row + held, :] = choose(z_v[row : row + held, :], value)

        together([ws[0][level - 1], ws[1][level - 1]], before_first if level == 1 else before_pivots, pivots)
        store(z_v.at[rows], front_out.at[rows])
        if last:
            break

        def prepare_next(level=level, row=piv_row, held=held):
            widen(m_v, ms_v, row + held, HELD[level])
            if level + 1 < LEVELS:
                widen(e_v, es_v, row + held, HELD[level])
            fill(level + 1)

        def updates(stream, level=level, row=piv_row, held=held):
            gather = zs[stream][level - 1]
            chunks = [
                operand(gather.buf[y, z].reshape(4 * held, N), min(held, B))
                for y in range(YS[level - 1])
                for z in range(ZS[level - 1])
            ]
            value = pack(multiply(es_v, row, held, chunks), min(held, B))
            send_update(stream, level, update_rows(stream, level) - value)

        together([zs[0][level - 1], zs[1][level - 1]], prepare_next, updates)
        piv_row += held

    spare = b_v.reshape(SB * B, N)
    for gather in gathers:
        gather.drain(spare)
    for copy in stores:
        copy.wait()


def tables(sub_pattern, sub_map, front_map):
    leaf = lax.axis_index("leaf")
    front = lax.axis_index("front")
    pivots = jnp.arange(PB, dtype=jnp.int32)
    places, flags = [], []
    maps = lax.dynamic_slice_in_dim(sub_map, leaf * 8, 8)
    wanted = jnp.concatenate([pivots, PB + 2 * front + jnp.arange(2, dtype=jnp.int32)])
    match = maps[None] == wanted[:, None, None]
    places.append(2 * jnp.arange(8, dtype=jnp.int32) + match[:, :, 1].astype(jnp.int32))
    flags.append(match.any(axis=2))
    for level in range(2, LEVELS + 1):
        held = HELD[level - 1]
        maps = lax.dynamic_slice_in_dim(
            front_map, MAP_AT[level - 2] + 2 * (leaf // 2 ** (level - 1)), 2
        )
        row = ((leaf % 2 ** (level - 1)) * 8 + front) * held
        wanted = jnp.concatenate([pivots, (PB + row // B)[None]])
        match = maps[None] == wanted[:, None, None]
        place = jnp.sum(match * jnp.arange(PB, dtype=jnp.int32), axis=2, dtype=jnp.int32)
        place = place + jnp.array([0, PB], jnp.int32)
        last = jnp.arange(PB + 1)[:, None] == PB
        unit = min(B, 2 * held)
        place = jnp.where(last, place * (B // unit) + row % B // unit, place)
        places.append(jnp.pad(place, ((0, 0), (0, 6))))
        flags.append(jnp.pad(match.any(axis=2), ((0, 0), (0, 6))))
    found = jnp.concatenate([jnp.concatenate(places), jnp.concatenate(flags).astype(jnp.int32)], axis=1)
    return jnp.concatenate([found, jnp.pad(sub_pattern[:, 1:], ((0, 0), (0, 15)))])


def per_device(
    sub_rhs, sub_dinv, sub_off, sub_pattern, sub_update, sub_map,
    front_rhs, piv_inverse, upd_factor, front_map,
):
    def wide(level, held):
        return pltpu.VMEM((YS[level - 1], ZS[level - 1], 4, 2, held, N), F32)

    scratch = [
        pltpu.VMEM((SB, B, N), F32),
        pltpu.VMEM((SB, B, B), F32),
        pltpu.VMEM((SB - 1, K, B, B), F32),
        pltpu.VMEM((2 * B, SB * B), F32),
        pltpu.VMEM((PROWS, ROWS), F32),
        pltpu.VMEM((UROWS, ROWS), F32),
        pltpu.VMEM((SB, B, N), F32),
        pltpu.VMEM((SB, B, 2 * N), BF16),
        pltpu.VMEM((2, 2 * B, 2 * B), BF16),
        pltpu.VMEM((2, B, N), F32),
        pltpu.VMEM((2 * B, N), F32),
        pltpu.VMEM((2, ROWS // 2, N), F32),
        pltpu.VMEM((ROWS, N), BF16),
        pltpu.VMEM((2 * PROWS, ROWS), BF16),
        pltpu.VMEM((2 * UROWS, ROWS), BF16),
        pltpu.VMEM((PROWS, N), F32),
    ]
    scratch += [wide(level, HELD[level - 1]) for level in range(1, 6)]
    for _ in range(2):
        scratch += [wide(1, B)]
        scratch += [wide(level + 1, HELD[level - 1] // 2) for level in range(1, 5)]
        scratch += [wide(level, HELD[level - 1] // 2) for level in range(1, 5)]
    copies = 3 * sum(SENDS) + 2 * sum(SENDS[:4]) + 23
    scratch += [
        pltpu.SemaphoreType.DMA((15,)),
        pltpu.SemaphoreType.DMA((6,)),
        pltpu.SemaphoreType.DMA((23,)),
        pltpu.SemaphoreType.DMA((copies,)),
    ]
    smem = pl.BlockSpec(memory_space=pltpu.SMEM)
    hbm = pl.BlockSpec(memory_space=pl.ANY)
    solved, fronts = pl.pallas_call(
        kernel,
        out_shape=(
            jax.ShapeDtypeStruct((SB, B, N), F32),
            jax.ShapeDtypeStruct((PROWS, N), F32),
        ),
        in_specs=[smem] + [hbm] * 7,
        out_specs=(hbm, hbm),
        scratch_shapes=scratch,
        compiler_params=pltpu.CompilerParams(
            collective_id=0, has_side_effects=True, vmem_limit_bytes=62 * 2**20
        ),
    )(
        tables(sub_pattern, sub_map, front_map),
        sub_rhs.reshape(SB, B, N), sub_dinv, sub_off, sub_update, front_rhs, piv_inverse, upd_factor,
    )
    return solved.reshape(SB * B, N), fronts


def solution(mesh):
    rows = P(("leaf", "front"), None)
    return jax.shard_map(
        per_device,
        mesh=mesh,
        in_specs=(
            rows,
            P(("leaf", "front"), None, None),
            P(("leaf", "front"), None, None, None),
            rows,
            rows,
            P(),
            rows,
            rows,
            rows,
            P(),
        ),
        out_specs=(rows, rows),
        check_vma=False,
    )
```
